32 devices in a mesh: str: 8 (over z, x), fac: 4 (over y, core).
Axes of the slice: x: 2, y: 2, z: 4, core: 2. Of those that a mesh axis runs over, the one named last changes fastest.
Arguments:
- amplitudes: bfloat16 [2, 4096, 4096], P(None, 'str'), may hold values from -6 to 6
- beta_index: int32 [2, 32, 12], replicated, may hold values from 0 to 31, all different within a row; in each aligned block of 32 rows (0 to 31, 32 to 63, ..., all dimensions but the last counted through in order) at most 24 rows name the same one
- beta_tile: int32 [2, 12], replicated, may hold values from 0 to 15
- beta_flip: int32 [2, 4096], replicated, may hold values 0 or 1
- alpha_index: int32 [2, 32, 12], replicated, may hold values from 0 to 31, all different within a row; in each aligned block of 32 rows (0 to 31, 32 to 63, ..., all dimensions but the last counted through in order) at most 24 rows name the same one
- alpha_tile: int32 [2, 12], replicated, may hold values from 0 to 15
- alpha_flip: int32 [2, 4096], replicated, may hold values 0 or 1
- beta_tiles: bfloat16 [16, 128, 128], replicated, may hold values from -0.15625 to 0.15625
- alpha_tiles: bfloat16 [16, 128, 128], replicated, may hold values from -0.109375 to 0.109375
Outputs:
- sigma: float32 [2, 4096, 4096], P(None, 'fac', 'str')
The draws below stay inside these ranges and needn't reach their ends.
Inputs may be any that keep to these rules, and one draw needn't show every extreme that they name: `beta_index`: each block row of one factor's beta operator names 12 different block columns; within one factor's operator no block column is named by more than 24 block rows, and in some factor one column is named by exactly 24. `alpha_index`: each block row of one factor's alpha operator names 12 different block columns; within one factor's operator no block column is named by more than 24 block rows, and in some factor one column is named by exactly 24.
All inputs are finite; a program needn't handle non-finite values.
Results may differ from the reference program's by a relative error of at most 0.012.
Values may be sent and summed in bfloat16 or wider, within the bound.
A program may use at most 128 MiB of HBM per device.

```python
import math
import jax
import jax.numpy as jnp
import numpy as np
from jax import lax

STRINGS = 4096
TILE = 128
KSLOT = 12
NTILE = 16
MOSTREF = 24
NBLK = 32
NFAC = 2


def set_ends(array, key, least, top_value):
    place = [jax.random.randint(jax.random.fold_in(key, axis), (), 0, length) for axis, length in enumerate(array.shape)]
    main_axis = array.shape.index(max(array.shape))
    beside = place[:main_axis] + [(place[main_axis] + 1) % array.shape[main_axis]] + place[main_axis + 1:]
    return array.at[tuple(place)].set(least).at[tuple(beside)].set(top_value)


def shard_levels(stream_key, dims, cuts, least, top_value):
    factor_of, own = 1.0, jax.random.fold_in(stream_key, 6)
    for axis_at, blocks in cuts:
        steps = jnp.exp(jax.random.uniform(jax.random.fold_in(own, axis_at), (blocks,), jnp.float32, least / len(cuts), top_value / len(cuts)))
        factor_of = factor_of * jnp.repeat(steps, dims[axis_at] // blocks).reshape([-1 if axis == axis_at else 1 for axis in range(len(dims))])
    return factor_of


def shared_out(key, own, number, rows, number_of, top, most, lean):
    order = jax.random.permutation(key, number_of)
    packed, ordinary = portions_of(number_of, rows * top, most, lean, True), portions_of(number_of, rows * top, most, lean, False)
    places = jnp.arange(number_of)

    def named(sizes, offset_by):
        used = int((sizes > 0).sum())
        fixed = max(1, used // 4)
        shifted = fixed + (places - fixed + offset_by * (used - fixed)) % max(1, number_of - fixed)
        return jnp.zeros((number_of,), jnp.int32).at[order[jnp.where(places < fixed, places, shifted)]].set(jnp.asarray(sizes, jnp.int32))

    sizes = jnp.where(number % 4 == 0, named(packed, number // 4), named(ordinary, number - number // 4 - 1))
    mixed = jax.random.permutation(jax.random.fold_in(own, 3), number_of)
    giver, receiver = mixed[0:number_of // 2 * 2:2], mixed[1:number_of // 2 * 2:2]
    slack = jnp.minimum(sizes[giver] - 1, most - sizes[receiver]) // 2
    slack = jnp.where((giver == order[0]) | (receiver == order[0]) | (sizes[receiver] == 0), 0, jnp.maximum(slack, 0))
    shifted = jax.random.randint(jax.random.fold_in(own, 4), (number_of // 2,), 0, 1 << 20) % (slack + 1)
    sizes = sizes.at[giver].add(-shifted).at[receiver].add(shifted)
    members = jnp.searchsorted(jnp.cumsum(sizes), jnp.arange(rows * top), side="right").astype(jnp.int32)
    listing = members.reshape(top, rows).T
    listing = listing[jax.random.permutation(jax.random.fold_in(own, 1), rows)]
    offset_by = jax.random.randint(jax.random.fold_in(own, 2), (rows, 1), 0, top)
    return jnp.take_along_axis(listing, (jnp.arange(top)[None, :] + offset_by) % top, axis=1)


def portions_of(count, total, limit, skew, full):
    weights = [(1 << 20) // math.isqrt(standing ** skew) + 1 for standing in range(1, count + 1)]
    largest = limit if full else min(limit, max(-(-total // count), total * weights[0] // sum(weights)))
    least = 1 if total - largest >= count - 1 else 0
    counts, surplus = [largest] + [least] * (count - 1), total - largest - least * (count - 1)
    while surplus > 0:
        free = [i for i in range(1, count) if counts[i] < largest] or [i for i in range(1, count) if counts[i] < limit]
        pool, budget = sum([weights[i] for i in free]), surplus
        for i in free:
            extra = min(limit - counts[i], max(1, budget * weights[i] // pool), surplus)
            counts[i] = counts[i] + extra
            surplus = surplus - extra
    return np.array(counts)


def scatter_about(rng, shape, scale, reach, cuts=(), held_as=jnp.bfloat16):
    level = shard_levels(rng, shape, cuts, -0.22, 0.18) if cuts else 1.0
    values = jax.random.normal(rng, shape, jnp.float32) * scale * level
    return jnp.minimum(jnp.maximum(values, -reach), reach).astype(held_as)


def setup_inputs(seed: int = 0) -> dict:
    keys = jax.random.split(jax.random.key(seed), 10)
    amplitudes = scatter_about(keys[0], (2, STRINGS, STRINGS), 1.0, 6.0, ((1, 8),))
    beta_index_keys = jax.random.split(jax.random.fold_in(keys[1], 1), NFAC * NBLK // NBLK)
    beta_index_turns = jax.random.permutation(jax.random.fold_in(keys[1], 3), NFAC * NBLK // NBLK)
    beta_index = jax.vmap(lambda own, number: shared_out(jax.random.fold_in(keys[1], 2), own, number, NBLK, NBLK, KSLOT, MOSTREF, 2))(beta_index_keys, beta_index_turns).reshape((NFAC, NBLK, KSLOT))
    beta_tile = set_ends(jax.random.randint(keys[2], (NFAC, KSLOT), 0, NTILE), jax.random.fold_in(keys[2], 1), 0, NTILE - 1).astype(jnp.int32)
    beta_flip = set_ends((jax.random.randint(keys[3], (NFAC, STRINGS), 0, 2) < 1).astype(jnp.int32), jax.random.fold_in(keys[3], 1), 0, 1)
    alpha_index_keys = jax.random.split(jax.random.fold_in(keys[4], 1), NFAC * NBLK // NBLK)
    alpha_index_turns = jax.random.permutation(jax.random.fold_in(keys[4], 3), NFAC * NBLK // NBLK)
    alpha_index = jax.vmap(lambda own, number: shared_out(jax.random.fold_in(keys[4], 2), own, number, NBLK, NBLK, KSLOT, MOSTREF, 2))(alpha_index_keys, alpha_index_turns).reshape((NFAC, NBLK, KSLOT))
    alpha_tile = set_ends(jax.random.randint(keys[5], (NFAC, KSLOT), 0, NTILE), jax.random.fold_in(keys[5], 1), 0, NTILE - 1).astype(jnp.int32)
    alpha_flip = set_ends((jax.random.randint(keys[6], (NFAC, STRINGS), 0, 2) < 1).astype(jnp.int32), jax.random.fold_in(keys[6], 1), 0, 1)
    beta_tiles = scatter_about(keys[7], (NTILE, TILE, TILE), (TILE * KSLOT) ** -0.5, 0.15625)
    alpha_tiles = scatter_about(keys[8], (NTILE, TILE, TILE), (TILE * KSLOT * NFAC) ** -0.5, 0.109375)
    return {"amplitudes": amplitudes, "beta_index": beta_index, "beta_tile": beta_tile, "beta_flip": beta_flip, "alpha_index": alpha_index, "alpha_tile": alpha_tile, "alpha_flip": alpha_flip, "beta_tiles": beta_tiles, "alpha_tiles": alpha_tiles}


def apply_beta(amplitudes, block_ids, tile_ids, flips, tile_table):
    part_count, height, column_count = amplitudes.shape
    tile_size = tile_table.shape[1]
    block_count = column_count // tile_size
    signs = (1 - 2 * flips).astype(jnp.bfloat16)
    signed = amplitudes * signs[None, None, :]
    blocks = signed.reshape(part_count, height, block_count, tile_size)
    weights = tile_table[tile_ids].astype(jnp.float32)
    group_size = block_count // 4
    pieces = []
    for group_id in range(4):
        lower = group_id * group_size
        chosen = block_ids[lower:lower + group_size]
        gathered = blocks[:, :, chosen].astype(jnp.float32)
        pieces.append(jnp.einsum("pajkc,krc->pajr", gathered, weights).astype(jnp.bfloat16))
    return jnp.concatenate(pieces, axis=2).reshape(part_count, height, column_count)


def apply_alpha(half, block_ids, tile_ids, flips, tile_table):
    part_count, total, column_count = half.shape
    tile_size = tile_table.shape[1]
    block_count = total // tile_size
    signs = (1 - 2 * flips).astype(jnp.bfloat16)
    signed = half * signs[None, :, None]
    blocks = signed.reshape(part_count, block_count, tile_size, column_count)
    weights = tile_table[tile_ids].astype(jnp.float32)
    group_size = block_count // 4
    pieces = []
    for group_id in range(4):
        lower = group_id * group_size
        chosen = block_ids[lower:lower + group_size]
        gathered = blocks[:, chosen].astype(jnp.float32)
        pieces.append(jnp.einsum("pjkcn,krc->pjrn", gathered, weights).astype(jnp.bfloat16))
    return jnp.concatenate(pieces, axis=1).reshape(part_count, total, column_count)


def reference(amplitudes, beta_index, beta_tile, beta_flip, alpha_index, alpha_tile, alpha_flip, beta_tiles, alpha_tiles):
    def accumulate(factor, summed):
        half = apply_beta(amplitudes, beta_index[factor], beta_tile[factor], beta_flip[factor], beta_tiles)
        half = lax.optimization_barrier(half)
        rounded = apply_alpha(half, alpha_index[factor], alpha_tile[factor], alpha_flip[factor], alpha_tiles)
        rounded = lax.optimization_barrier(rounded)
        return summed + rounded.astype(jnp.float32)

    initial = jnp.zeros(amplitudes.shape, jnp.float32)
    return lax.fori_loop(0, NFAC, accumulate, initial)
```

```python
import functools
import math

import jax
import jax.numpy as jnp
from jax import lax
from jax.experimental import pallas as pl
from jax.experimental.pallas import tpu as pltpu
from jax.sharding import PartitionSpec as P

MESH = pl.DeviceIdType.MESH


def split_position(pos, F):
    factors = F // 2
    return pos % factors, pos // factors


def kernel(dims, amp_hbm, bflip_hbm, aflip_hbm, btab_hbm, atab_hbm, bidx_hbm, aidx_hbm, btile_hbm, atile_hbm, out, *scratch):
    S, F, C, A, T, K, NB, H = dims
    amp, half_send, term_send, pair_recv, wb, wa, bflip, aflip, btab, atab, sign_a, bidx, aidx, btile, atile, raw = scratch[:16]
    recv = scratch[16 : 16 + C]
    a_sem, t_sem, s_send, s_recv, p_send, p_recv, f_send, f_recv = scratch[16 + C :]
    me = lax.axis_index("str")
    pos = lax.axis_index("fac")
    fac, part = split_position(pos, F)
    chips = F // 2
    chip = pos // 2
    core = pos % 2
    per = term_send.shape[1] // F

    barrier = pltpu.get_barrier_semaphore()

    def greet_str(t, _):
        pl.semaphore_signal(barrier, inc=1, device_id={"str": (me + 1 + t) % S}, device_id_type=MESH)
        return 0

    def greet_fac(t, _):
        peer = ((chip + 1 + t) % chips) * 2 + core
        pl.semaphore_signal(barrier, inc=1, device_id={"fac": peer}, device_id_type=MESH)
        return 0

    partner = chip * 2 + 1 - core
    lax.fori_loop(0, S - 1, greet_str, 0)
    lax.fori_loop(0, chips - 1, greet_fac, 0)
    pl.semaphore_signal(barrier, inc=1, device_id={"fac": partner}, device_id_type=MESH)

    tables = [
        pltpu.make_async_copy(src, dst, t_sem.at[n])
        for n, (src, dst) in enumerate(
            [
                (bflip_hbm, bflip),
                (aflip_hbm, aflip),
                (btab_hbm, btab),
                (bidx_hbm, bidx),
                (btile_hbm, btile),
                (atab_hbm, atab),
                (aidx_hbm, aidx),
                (atile_hbm, atile),
            ]
        )
    ]

    strip = A * T // 8

    def load(k):
        return pltpu.make_async_copy(amp_hbm.at[part, pl.ds(k * strip, strip)], raw.at[pl.ds(k * strip, strip)], a_sem.at[k])

    def start_load(k, _):
        load(k).start()
        return 0

    for copy in tables[:5]:
        copy.start()
    lax.fori_loop(0, 8, start_load, 0)
    for copy in tables[5:]:
        copy.start()

    def signs(flips, block):
        value = flips[:, pl.ds(block * T if isinstance(block, int) else pl.multiple_of(block * T, T), T)].astype(jnp.float32)
        mine = lax.broadcasted_iota(jnp.int32, value.shape, 0) == fac
        return 1 - 2 * jnp.sum(jnp.where(mine, value, 0.0), axis=0, keepdims=True)

    tables[1].wait()
    for r in range(A):
        row = signs(aflip, me * A + r)
        sign_a[pl.ds(r * T, T), :] = jnp.broadcast_to(row, (T, T)).T.astype(jnp.bfloat16)
    tables[4].wait()
    tables[2].wait()
    for s in range(K):
        wb[pl.ds(s * T, T), :] = btab[btile[fac, s]].T
    tables[0].wait()
    tables[3].wait()

    def sign(r, _):
        load(r).wait()
        rows = pl.ds(pl.multiple_of(r * strip, strip), strip)
        row_sign = sign_a[rows, :]
        for k in range(NB):
            amp[k, rows, :] = raw[rows, pl.ds(k * T, T)] * signs(bflip, k).astype(jnp.bfloat16) * row_sign
        return 0

    lax.fori_loop(0, 8, sign, 0)
    pl.semaphore_wait(barrier, S - 1 + chips)

    mid = S // 2

    def dest(t):
        side = (me // mid + 1 + t // mid) % 2
        return side * mid + (me + 1 + t) % mid

    def beta(q, c):
        j = q * C + c
        lhs = jnp.concatenate([amp[bidx[s, fac, j]] for s in range(K)], axis=1)
        res = jnp.dot(lhs, wb[...], preferred_element_type=jnp.float32)
        return res.astype(jnp.bfloat16).reshape(A, T, T)

    def str_copy(c, q, src):
        return pltpu.make_async_remote_copy(
            src_ref=half_send.at[c, q],
            dst_ref=recv[c].at[pl.ds(src * A, A)],
            send_sem=s_send.at[c, q],
            recv_sem=s_recv.at[c, src],
            device_id={"str": q},
            device_id_type=MESH,
        )

    for c in range(C):

        def step(t, _):
            q = dest(t)
            half_send[c, q] = beta(q, c)
            str_copy(c, q, me).start()
            return 0

        lax.fori_loop(0, S - 1, step, 0)
        recv[c][pl.ds(me * A, A)] = beta(me, c)

    for copy in tables[5:]:
        copy.wait()
    for s in range(K):
        wa[:, pl.ds(s * T, T)] = atab[atile[fac, s]]

    piece = per // H
    groups = chips * H

    def place(g):
        return (chip + 1 + g // H) % chips, g % H

    def pair_copy(c, y, h, owner):
        return pltpu.make_async_remote_copy(
            src_ref=term_send.at[c, pl.ds((y * 2 + owner) * per + h * piece, piece)],
            dst_ref=pair_recv.at[c, y, h],
            send_sem=p_send.at[c, y, h],
            recv_sem=p_recv.at[c, y, h],
            device_id={"fac": partner},
            device_id_type=MESH,
        )

    def fac_copy(c, y, h, src):
        src_fac, src_part = split_position(src, F)
        return pltpu.make_async_remote_copy(
            src_ref=term_send.at[c, pl.ds((y * 2 + core) * per + h * piece, piece)],
            dst_ref=out.at[src_fac // 2, src_part, pl.ds(h * piece, piece), pl.ds(c * T, T)],
            send_sem=f_send.at[c, y, h],
            recv_sem=f_recv.at[c, src // 2, h],
            device_id={"fac": y * 2 + core},
            device_id_type=MESH,
        )

    def own_copy(c):
        return pltpu.make_async_copy(
            term_send.at[c, pl.ds(pos * per, per)],
            out.at[fac // 2, part, :, pl.ds(c * T, T)],
            f_send.at[c, chip, 0],
        )

    for c in range(C):

        def arrive(t, _):
            src = (me + 1 + t) % S
            str_copy(c, src, src).wait_recv()
            return 0

        lax.fori_loop(0, S - 1, arrive, 0)

        def alpha(i):
            rhs = jnp.concatenate([recv[c][aidx[s, fac, i]] for s in range(K)], axis=0)
            return jnp.dot(wa[...], rhs, preferred_element_type=jnp.float32)

        def store(i, value):
            term_send[c, pl.ds(pl.multiple_of(i * T, T), T), :] = value.astype(jnp.bfloat16)

        def for_partner(g):
            y, h = place(g)

            def block(b, _):
                i = (y * 2 + 1 - core) * (per // T) + h * (piece // T) + b
                store(i, alpha(i))
                return 0

            lax.fori_loop(0, piece // T, block, 0)
            pair_copy(c, y, h, 1 - core).start()

        def for_self(g):
            y, h = place(g)
            pair_copy(c, y, h, core).wait_recv()

            def block(b, _):
                i = (y * 2 + core) * (per // T) + h * (piece // T) + b
                other = pair_recv[c, y, h, pl.ds(pl.multiple_of(b * T, T), T), :]
                store(i, alpha(i) + other.astype(jnp.float32))
                return 0

            lax.fori_loop(0, piece // T, block, 0)

        def away(g, _):
            for_partner(g + 1)
            for_self(g)
            y, h = place(g)
            fac_copy(c, y, h, pos).start()
            return 0

        def home(g, _):
            for_partner(g + 1)
            for_self(g)
            return 0

        for_partner(0)
        lax.fori_loop(0, groups - H, away, 0)
        lax.fori_loop(groups - H, groups - 1, home, 0)
        for_self(groups - 1)
        own_copy(c).start()

    for c in range(C):

        def finish_str(t, _):
            str_copy(c, (me + 1 + t) % S, me).wait_send()
            return 0

        lax.fori_loop(0, S - 1, finish_str, 0)

        def finish_pair(g, _):
            y, h = place(g)
            pair_copy(c, y, h, 1 - core).wait_send()
            return 0

        lax.fori_loop(0, groups, finish_pair, 0)

        def finish_fac(g, _):
            y, h = place(g)
            fac_copy(c, y, h, pos).wait_send()
            fac_copy(c, y, h, y * 2 + core).wait_recv()
            return 0

        lax.fori_loop(0, groups - H, finish_fac, 0)
        own_copy(c).wait()


def local(S, F, amplitudes, beta_index, beta_tile, beta_flip, alpha_index, alpha_tile, alpha_flip, beta_tiles, alpha_tiles):
    NF, NB, K = beta_index.shape
    NT, T, _ = beta_tiles.shape
    parts, height, width = amplitudes.shape
    total = height * S
    A = height // T
    C = width // S // T
    assert F == 2 * NF and parts == 2 and NF % 2 == 0 and height % 128 == 0
    per = total // F
    H = math.gcd(per // T, 4)
    ids = (beta_index.transpose(2, 0, 1), alpha_index.transpose(2, 0, 1), beta_tile, alpha_tile)
    hbm = pl.BlockSpec(memory_space=pltpu.HBM)
    bf16 = jnp.bfloat16
    dma = pltpu.SemaphoreType.DMA
    terms = pl.pallas_call(
        functools.partial(kernel, (S, F, C, A, T, K, NB, H)),
        out_shape=jax.ShapeDtypeStruct((NF // 2, parts, per, width // S), bf16),
        in_specs=[hbm] * 9,
        out_specs=pl.BlockSpec(memory_space=pl.ANY),
        scratch_shapes=[
            pltpu.VMEM((NB, height, T), bf16),
            pltpu.VMEM((C, S, A, T, T), bf16),
            pltpu.VMEM((C, total, T), bf16),
            pltpu.VMEM((C, F // 2, H, per // H, T), bf16),
            pltpu.VMEM((K * T, T), bf16),
            pltpu.VMEM((T, K * T), bf16),
            pltpu.VMEM((NF, width), jnp.int32),
            pltpu.VMEM((NF, total), jnp.int32),
            pltpu.VMEM((NT, T, T), bf16),
            pltpu.VMEM((NT, T, T), bf16),
            pltpu.VMEM((height, T), bf16),
            pltpu.SMEM((K, NF, NB), jnp.int32),
            pltpu.SMEM((K, NF, NB), jnp.int32),
            pltpu.SMEM((NF, K), jnp.int32),
            pltpu.SMEM((NF, K), jnp.int32),
            pltpu.VMEM((height, width), bf16),
        ]
        + [pltpu.VMEM((NB, T, T), bf16) for _ in range(C)]
        + [dma((8,)), dma((8,)), dma((C, S)), dma((C, S))]
        + [dma((C, F // 2, H)) for _ in range(4)],
        compiler_params=pltpu.CompilerParams(collective_id=0, has_side_effects=True, vmem_limit_bytes=67043328),
        name="sigma",
    )(amplitudes, beta_flip, alpha_flip, beta_tiles, alpha_tiles, *ids)
    return jnp.sum(terms.astype(jnp.float32), axis=0)


def halves_kernel(dims, amp_hbm, bflip_hbm, aflip_hbm, btab_hbm, atab_hbm, bidx_hbm, aidx_hbm, btile_hbm, atile_hbm, out, far_out, *scratch):
    S, F, C, A, T, K, NB, H = dims
    amp, half_send, term_send, pair_recv, wb, wa, bflip, aflip, btab, atab, sign_a, sign_b, bidx, aidx, btile, atile, raw = scratch[:17]
    recv = scratch[17 : 16 + C]
    part_recv = scratch[16 + C : 18 + C]
    a_sem, t_sem, s_send, s_recv, p_send, p_recv, f_send, f_recv, x_send, x_recv = scratch[18 + C :]
    me = lax.axis_index("str")
    pos = lax.axis_index("fac")
    fac, part = split_position(pos, F)
    chips = F // 2
    chip = pos // 2
    core = pos % 2
    partner = chip * 2 + 1 - core
    per = term_send.shape[1] // F
    mid = S // 2
    side = me // mid
    first = side * mid
    mirror = (1 - side) * mid + me % mid
    last = C - 1

    def far(t):
        return (1 - side) * mid + (me + t) % mid

    def near(t):
        return first + (me + 1 + t) % mid

    barrier = pltpu.get_barrier_semaphore()

    def greet_str(t, _):
        pl.semaphore_signal(barrier, inc=1, device_id={"str": (me + 1 + t) % S}, device_id_type=MESH)
        return 0

    def greet_fac(t, _):
        peer = ((chip + 1 + t) % chips) * 2 + core
        pl.semaphore_signal(barrier, inc=1, device_id={"fac": peer}, device_id_type=MESH)
        pl.semaphore_signal(barrier, inc=1, device_id={"str": mirror, "fac": peer}, device_id_type=MESH)
        return 0

    lax.fori_loop(0, S - 1, greet_str, 0)
    lax.fori_loop(0, chips - 1, greet_fac, 0)
    pl.semaphore_signal(barrier, inc=1, device_id={"fac": partner}, device_id_type=MESH)

    tables = [
        pltpu.make_async_copy(src, dst, t_sem.at[n])
        for n, (src, dst) in enumerate(
            [
                (bflip_hbm, bflip),
                (aflip_hbm, aflip),
                (btile_hbm, btile),
                (bidx_hbm, bidx),
                (btab_hbm, btab),
                (atab_hbm, atab),
                (aidx_hbm, aidx),
                (atile_hbm, atile),
            ]
        )
    ]

    def load(a):
        return pltpu.make_async_copy(amp_hbm.at[part, pl.ds(a * T, T)], raw.at[pl.ds(a * T, T)], a_sem.at[a])

    for copy in tables[:5]:
        copy.start()
    for a in range(A):
        load(a).start()
    for copy in tables[5:]:
        copy.start()

    def signs(flips, start, size):
        value = flips[:, pl.ds(start, size)]
        mine = lax.broadcasted_iota(jnp.int32, value.shape, 0) == fac
        return 1 - 2 * jnp.sum(jnp.where(mine, value.astype(jnp.float32), 0.0), axis=0, keepdims=True)

    tables[0].wait()
    sign_b[...] = jnp.broadcast_to(signs(bflip, 0, NB * T), sign_b.shape).astype(jnp.bfloat16)
    tables[1].wait()
    for a in range(A):
        row = signs(aflip, pl.multiple_of((me * A + a) * T, T), T)
        sign_a[pl.ds(a * T, T), :] = jnp.broadcast_to(row, (T, T)).T.astype(jnp.bfloat16)
    tables[2].wait()
    tables[3].wait()
    tables[4].wait()
    for s in range(K):
        wb[pl.ds(s * T, T), :] = btab[btile[fac, s]].T
    for m in range(2):
        part_recv[m][mid * A] = jnp.zeros((T, T), jnp.bfloat16)

    def str_copy(c, q, src):
        return pltpu.make_async_remote_copy(
            src_ref=half_send.at[c, q],
            dst_ref=recv[c].at[pl.ds(src * A, A)],
            send_sem=s_send.at[c, q],
            recv_sem=s_recv.at[c, src],
            device_id={"str": q},
            device_id_type=MESH,
        )

    def strip_copy(q, a):
        return pltpu.make_async_remote_copy(
            src_ref=half_send.at[0, q, a],
            dst_ref=recv[0].at[me * A + a],
            send_sem=s_send.at[0, q],
            recv_sem=s_recv.at[0, me],
            device_id={"str": q},
            device_id_type=MESH,
        )

    def owner(m, r):
        return r if m == 0 else (1 - side) * mid + r % mid

    def part_copy(m, r, src):
        return pltpu.make_async_remote_copy(
            src_ref=half_send.at[last, owner(m, r)],
            dst_ref=part_recv[m].at[pl.ds(src % mid * A, A)],
            send_sem=s_send.at[last, owner(m, r)],
            recv_sem=s_recv.at[last, m * mid + src % mid],
            device_id={"str": r},
            device_id_type=MESH,
        )

    def sign(a):
        load(a).wait()
        rows = pl.ds(pl.multiple_of(a * T, T), T)
        row_sign = sign_a[rows, :]
        for k in range(NB):
            column = jnp.broadcast_to(sign_b[:, k * T : (k + 1) * T].reshape(1, 16, T), (T // 16, 16, T)).reshape(T, T)
            amp[k, rows, :] = raw[rows, k * T : (k + 1) * T] * column * row_sign

    def strip(a):
        rows = pl.ds(pl.multiple_of(a * T, T), T)
        blocks = [jnp.concatenate([amp[bidx[s, fac, far(t) * C], rows, :] for s in range(K)], axis=1) for t in range(mid)]
        res = jnp.dot(jnp.concatenate(blocks, axis=0), wb[...], preferred_element_type=jnp.float32).astype(jnp.bfloat16)
        for t in range(mid):
            half_send[0, far(t), a] = res[t * T : (t + 1) * T]

    def send_strip(a):
        for t in range(mid):
            strip_copy(far(t), a).start()

    sign(0)
    strip(0)
    pl.semaphore_wait(barrier, S - 1 + 2 * chips - 1)
    send_strip(0)

    def each_strip(a, _):
        sign(a)
        strip(a)
        send_strip(a)
        return 0

    lax.fori_loop(1, A, each_strip, 0)

    def beta(j):
        lhs = jnp.concatenate([amp[bidx[s, fac, j]] for s in range(K)], axis=1)
        res = jnp.dot(lhs, wb[...], preferred_element_type=jnp.float32)
        return res.astype(jnp.bfloat16).reshape(A, T, T)

    for m in (1, 0):

        def near_part(t, _):
            r = near(t)
            half_send[last, owner(m, r)] = beta(owner(m, r) * C + last)
            part_copy(m, r, me).start()
            return 0

        lax.fori_loop(0, mid - 1, near_part, 0)
        part_recv[m][pl.ds(me % mid * A, A)] = beta(owner(m, me) * C + last)

    for c in range(last):

        def to_far(t, _):
            q = far(t)
            half_send[c, q] = beta(q * C + c)
            str_copy(c, q, me).start()
            return 0

        def to_near(t, _):
            q = near(t)
            half_send[c, q] = beta(q * C + c)
            str_copy(c, q, me).start()
            return 0

        if c > 0:
            lax.fori_loop(0, mid, to_far, 0)
        lax.fori_loop(0, mid - 1, to_near, 0)
        recv[c][pl.ds(me * A, A)] = beta(me * C + c)

    for copy in tables[5:]:
        copy.wait()
    for s in range(K):
        wa[:, pl.ds(s * T, T)] = atab[atile[fac, s]]

    piece = per // H
    groups = chips * H

    def place(g):
        return (chip + 1 + g // H) % chips, g % H

    def pair_copy(u, y, h, owner_core):
        return pltpu.make_async_remote_copy(
            src_ref=term_send.at[u, pl.ds((y * 2 + owner_core) * per + h * piece, piece)],
            dst_ref=pair_recv.at[u, y, h],
            send_sem=p_send.at[u, y, h],
            recv_sem=p_recv.at[u, y, h],
            device_id={"fac": partner},
            device_id_type=MESH,
        )

    def fac_copy(c, y, h, src):
        src_fac, src_part = split_position(src, F)
        return pltpu.make_async_remote_copy(
            src_ref=term_send.at[c, pl.ds((y * 2 + core) * per + h * piece, piece)],
            dst_ref=out.at[src_fac // 2, src_part, pl.ds(h * piece, piece), pl.ds(c * T, T)],
            send_sem=f_send.at[c, y, h],
            recv_sem=f_recv.at[c, src // 2, h],
            device_id={"fac": y * 2 + core},
            device_id_type=MESH,
        )

    def far_copy(y, h, src):
        src_fac, src_part = split_position(src, F)
        return pltpu.make_async_remote_copy(
            src_ref=term_send.at[C, pl.ds((y * 2 + core) * per + h * piece, piece)],
            dst_ref=far_out.at[src_fac // 2, src_part, pl.ds(h * piece, piece)],
            send_sem=x_send.at[y, h],
            recv_sem=x_recv.at[src // 2, h],
            device_id={"str": mirror, "fac": y * 2 + core},
            device_id_type=MESH,
        )

    def own_copy(c):
        return pltpu.make_async_copy(
            term_send.at[c, pl.ds(pos * per, per)],
            out.at[fac // 2, part, :, pl.ds(c * T, T)],
            f_send.at[c, chip, 0],
        )

    def stage(u, gather, send, sent):
        def alpha(i):
            return jnp.dot(wa[...], gather(i), preferred_element_type=jnp.float32)

        def store(i, value):
            term_send[u, pl.ds(pl.multiple_of(i * T, T), T), :] = value.astype(jnp.bfloat16)

        def for_partner(g):
            y, h = place(g)

            def block(b, _):
                i = (y * 2 + 1 - core) * (per // T) + h * (piece // T) + b
                store(i, alpha(i))
                return 0

            lax.fori_loop(0, piece // T, block, 0)
            pair_copy(u, y, h, 1 - core).start()

        def for_self(g):
            y, h = place(g)
            pair_copy(u, y, h, core).wait_recv()

            def block(b, _):
                i = (y * 2 + core) * (per // T) + h * (piece // T) + b
                other = pair_recv[u, y, h, pl.ds(pl.multiple_of(b * T, T), T), :]
                store(i, alpha(i) + other.astype(jnp.float32))
                return 0

            lax.fori_loop(0, piece // T, block, 0)

        def away(g, _):
            for_partner(g + 1)
            for_self(g)
            y, h = place(g)
            send(y, h).start()
            return 0

        def home(g, _):
            for_partner(g + 1)
            for_self(g)
            return 0

        for_partner(0)
        if sent == groups:
            lax.fori_loop(0, groups - 1, away, 0)
            for_self(groups - 1)
            y, h = place(groups - 1)
            send(y, h).start()
        else:
            lax.fori_loop(0, sent, away, 0)
            lax.fori_loop(sent, groups - 1, home, 0)
            for_self(groups - 1)

    def gather_part(m):
        def gather(i):
            blocks = []
            for s in range(K):
                k = aidx[s, fac, i] - first * A
                blocks.append(part_recv[m][jnp.where((k >= 0) & (k < mid * A), k, mid * A)])
            return jnp.concatenate(blocks, axis=0)

        return gather

    def gather_full(c):
        return lambda i: jnp.concatenate([recv[c][aidx[s, fac, i]] for s in range(K)], axis=0)

    for m in (1, 0):

        def arrive_part(t, _):
            part_copy(m, me, near(t)).wait_recv()
            return 0

        lax.fori_loop(0, mid - 1, arrive_part, 0)
        if m == 1:
            stage(C, gather_part(1), lambda y, h: far_copy(y, h, pos), groups)
        else:
            stage(last, gather_part(0), lambda y, h: fac_copy(last, y, h, pos), groups - H)
            own_copy(last).start()

    for c in range(last):

        def arrive(t, _):
            src = (me + 1 + t) % S
            str_copy(c, src, src).wait_recv()
            return 0

        lax.fori_loop(0, S - 1, arrive, 0)
        stage(c, gather_full(c), lambda y, h: fac_copy(c, y, h, pos), groups - H)
        own_copy(c).start()

    for c in range(last):

        def finish_str(t, _):
            str_copy(c, (me + 1 + t) % S, me).wait_send()
            return 0

        lax.fori_loop(0, S - 1, finish_str, 0)

    for m in range(2):

        def finish_part(t, _):
            part_copy(m, near(t), me).wait_send()
            return 0

        lax.fori_loop(0, mid - 1, finish_part, 0)

    for u in range(C + 1):

        def finish_pair(g, _):
            y, h = place(g)
            pair_copy(u, y, h, 1 - core).wait_send()
            return 0

        lax.fori_loop(0, groups, finish_pair, 0)

    for c in range(C):

        def finish_fac(g, _):
            y, h = place(g)
            fac_copy(c, y, h, pos).wait_send()
            fac_copy(c, y, h, y * 2 + core).wait_recv()
            return 0

        lax.fori_loop(0, groups - H, finish_fac, 0)
        own_copy(c).wait()

    def finish_far(g, _):
        y, h = place(g)
        far_copy(y, h, pos).wait_send()
        far_copy(y, h, y * 2 + core).wait_recv()
        return 0

    lax.fori_loop(0, groups, finish_far, 0)


def finish_kernel(T, rows, terms, far, out, wide, sem):
    slots, parts, per, width = terms.shape
    count = per // rows

    def copy(p, r):
        block = pl.ds(pl.multiple_of(r * rows, rows), rows)
        return pltpu.make_async_copy(wide.at[p, block], out.at[p, block], sem.at[p, r])

    for p in range(parts):

        def convert(r, _):
            block = pl.ds(pl.multiple_of(r * rows, rows), rows)
            value = sum(terms[n, p, block, :].astype(jnp.float32) for n in range(slots))
            tail = sum(far[n, p, block, :].astype(jnp.float32) for n in range(slots))
            wide[p, block, : width - T] = value[:, : width - T]
            wide[p, block, width - T :] = value[:, width - T :] + tail
            copy(p, r).start()
            return 0

        lax.fori_loop(0, count, convert, 0)

    for p in range(parts):

        def wait(r, _):
            copy(p, r).wait()
            return 0

        lax.fori_loop(0, count, wait, 0)


def halves(S, F, amplitudes, beta_index, beta_tile, beta_flip, alpha_index, alpha_tile, alpha_flip, beta_tiles, alpha_tiles):
    NF, NB, K = beta_index.shape
    NT, T, _ = beta_tiles.shape
    parts, height, width = amplitudes.shape
    total = height * S
    A = height // T
    C = width // S // T
    mid = S // 2
    assert F == 2 * NF and parts == 2 and NF % 2 == 0 and height % T == 0 and S % 2 == 0
    per = total // F
    H = math.gcd(per // T, 4)
    ids = (beta_index.transpose(2, 0, 1), alpha_index.transpose(2, 0, 1), beta_tile, alpha_tile)
    hbm = pl.BlockSpec(memory_space=pltpu.HBM)
    vmem = pl.BlockSpec(memory_space=pltpu.VMEM)
    bf16 = jnp.bfloat16
    dma = pltpu.SemaphoreType.DMA
    terms, far = pl.pallas_call(
        functools.partial(halves_kernel, (S, F, C, A, T, K, NB, H)),
        out_shape=(
            pltpu.VMEM((NF // 2, parts, per, width // S), bf16),
            pltpu.VMEM((NF // 2, parts, per, T), bf16),
        ),
        in_specs=[hbm] * 9,
        out_specs=(vmem, vmem),
        scratch_shapes=[
            pltpu.VMEM((NB, height, T), bf16),
            pltpu.VMEM((C, S, A, T, T), bf16),
            pltpu.VMEM((C + 1, total, T), bf16),
            pltpu.VMEM((C + 1, F // 2, H, per // H, T), bf16),
            pltpu.VMEM((K * T, T), bf16),
            pltpu.VMEM((T, K * T), bf16),
            pltpu.VMEM((NF, width), jnp.int32),
            pltpu.VMEM((NF, total), jnp.int32),
            pltpu.VMEM((NT, T, T), bf16),
            pltpu.VMEM((NT, T, T), bf16),
            pltpu.VMEM((height, T), bf16),
            pltpu.VMEM((16, width), bf16),
            pltpu.SMEM((K, NF, NB), jnp.int32),
            pltpu.SMEM((K, NF, NB), jnp.int32),
            pltpu.SMEM((NF, K), jnp.int32),
            pltpu.SMEM((NF, K), jnp.int32),
            pltpu.VMEM((height, width), bf16),
        ]
        + [pltpu.VMEM((NB, T, T), bf16) for _ in range(C - 1)]
        + [pltpu.VMEM((mid * A + 1, T, T), bf16) for _ in range(2)]
        + [dma((A,)), dma((8,)), dma((C, S)), dma((C, S))]
        + [dma((C + 1, F // 2, H)) for _ in range(2)]
        + [dma((C, F // 2, H)) for _ in range(2)]
        + [dma((F // 2, H)) for _ in range(2)],
        compiler_params=pltpu.CompilerParams(collective_id=0, has_side_effects=True, vmem_limit_bytes=48 << 20),
        name="sigma",
    )(*[pltpu.with_memory_space_constraint(x, pltpu.HBM) for x in (amplitudes, beta_flip, alpha_flip, beta_tiles, alpha_tiles, *ids)])
    rows = math.gcd(per, 128)
    return pl.pallas_call(
        functools.partial(finish_kernel, T, rows),
        out_shape=jax.ShapeDtypeStruct((parts, per, width // S), jnp.float32),
        in_specs=[vmem, vmem],
        out_specs=pl.BlockSpec(memory_space=pltpu.HBM),
        scratch_shapes=[pltpu.VMEM((parts, per, width // S), jnp.float32), dma((parts, per // rows))],
        compiler_params=pltpu.CompilerParams(vmem_limit_bytes=16 << 20),
        name="finish",
    )(terms, far)


def either(S, F, *args):
    height, width, T = args[0].shape[1], args[0].shape[2], args[7].shape[1]
    form = halves if width // S >= 2 * T and height % T == 0 and S % 2 == 0 else local
    return form(S, F, *args)


def solution(mesh):
    return jax.shard_map(
        functools.partial(either, mesh.shape["str"], mesh.shape["fac"]),
        mesh=mesh,
        in_specs=(P(None, "str", None), P(), P(), P(), P(), P(), P(), P(), P()),
        out_specs=P(None, "fac", "str"),
        check_vma=False,
    )
```

```python
import functools
import math

import jax
import jax.numpy as jnp
from jax import lax
from jax.experimental import pallas as pl
from jax.experimental.pallas import tpu as pltpu
from jax.sharding import PartitionSpec as P

MESH = pl.DeviceIdType.MESH


def split_position(pos, F):
    factors = F // 2
    return pos % factors, pos // factors


def kernel(dims, amp_hbm, bflip_hbm, aflip_hbm, btab_hbm, atab_hbm, bidx_hbm, aidx_hbm, btile_hbm, atile_hbm, out, *scratch):
    S, F, C, A, T, K, NB, H = dims
    amp, half_send, term_send, pair_recv, wb, wa, bflip, aflip, btab, atab, sign_a, bidx, aidx, btile, atile, raw = scratch[:16]
    recv = scratch[16 : 16 + C]
    a_sem, t_sem, s_send, s_recv, p_send, p_recv, f_send, f_recv = scratch[16 + C :]
    me = lax.axis_index("str")
    pos = lax.axis_index("fac")
    fac, part = split_position(pos, F)
    chips = F // 2
    chip = pos // 2
    core = pos % 2
    per = term_send.shape[1] // F

    barrier = pltpu.get_barrier_semaphore()

    def greet_str(t, _):
        pl.semaphore_signal(barrier, inc=1, device_id={"str": (me + 1 + t) % S}, device_id_type=MESH)
        return 0

    def greet_fac(t, _):
        peer = ((chip + 1 + t) % chips) * 2 + core
        pl.semaphore_signal(barrier, inc=1, device_id={"fac": peer}, device_id_type=MESH)
        return 0

    partner = chip * 2 + 1 - core
    lax.fori_loop(0, S - 1, greet_str, 0)
    lax.fori_loop(0, chips - 1, greet_fac, 0)
    pl.semaphore_signal(barrier, inc=1, device_id={"fac": partner}, device_id_type=MESH)

    tables = [
        pltpu.make_async_copy(src, dst, t_sem.at[n])
        for n, (src, dst) in enumerate(
            [
                (bflip_hbm, bflip),
                (aflip_hbm, aflip),
                (btab_hbm, btab),
                (bidx_hbm, bidx),
                (btile_hbm, btile),
                (atab_hbm, atab),
                (aidx_hbm, aidx),
                (atile_hbm, atile),
            ]
        )
    ]

    strip = A * T // 8

    def load(k):
        return pltpu.make_async_copy(amp_hbm.at[part, pl.ds(k * strip, strip)], raw.at[pl.ds(k * strip, strip)], a_sem.at[k])

    def start_load(k, _):
        load(k).start()
        return 0

    for copy in tables[:5]:
        copy.start()
    lax.fori_loop(0, 8, start_load, 0)
    for copy in tables[5:]:
        copy.start()

    def signs(flips, block):
        value = flips[:, pl.ds(block * T if isinstance(block, int) else pl.multiple_of(block * T, T), T)].astype(jnp.float32)
        mine = lax.broadcasted_iota(jnp.int32, value.shape, 0) == fac
        return 1 - 2 * jnp.sum(jnp.where(mine, value, 0.0), axis=0, keepdims=True)

    tables[1].wait()
    for r in range(A):
        row = signs(aflip, me * A + r)
        sign_a[pl.ds(r * T, T), :] = jnp.broadcast_to(row, (T, T)).T.astype(jnp.bfloat16)
    tables[4].wait()
    tables[2].wait()
    for s in range(K):
        wb[pl.ds(s * T, T), :] = btab[btile[fac, s]].T
    tables[0].wait()
    tables[3].wait()

    def sign(r, _):
        load(r).wait()
        rows = pl.ds(pl.multiple_of(r * strip, strip), strip)
        row_sign = sign_a[rows, :]
        for k in range(NB):
            amp[k, rows, :] = raw[rows, pl.ds(k * T, T)] * signs(bflip, k).astype(jnp.bfloat16) * row_sign
        return 0

    lax.fori_loop(0, 8, sign, 0)
    pl.semaphore_wait(barrier, S - 1 + chips)

    mid = S // 2

    def dest(t):
        side = (me // mid + 1 + t // mid) % 2
        return side * mid + (me + 1 + t) % mid

    def beta(q, c):
        j = q * C + c
        lhs = jnp.concatenate([amp[bidx[s, fac, j]] for s in range(K)], axis=1)
        res = jnp.dot(lhs, wb[...], preferred_element_type=jnp.float32)
        return res.astype(jnp.bfloat16).reshape(A, T, T)

    def str_copy(c, q, src):
        return pltpu.make_async_remote_copy(
            src_ref=half_send.at[c, q],
            dst_ref=recv[c].at[pl.ds(src * A, A)],
            send_sem=s_send.at[c, q],
            recv_sem=s_recv.at[c, src],
            device_id={"str": q},
            device_id_type=MESH,
        )

    for c in range(C):

        def step(t, _):
            q = dest(t)
            half_send[c, q] = beta(q, c)
            str_copy(c, q, me).start()
            return 0

        lax.fori_loop(0, S - 1, step, 0)
        recv[c][pl.ds(me * A, A)] = beta(me, c)

    for copy in tables[5:]:
        copy.wait()
    for s in range(K):
        wa[:, pl.ds(s * T, T)] = atab[atile[fac, s]]

    piece = per // H
    groups = chips * H

    def place(g):
        return (chip + 1 + g // H) % chips, g % H

    def pair_copy(c, y, h, owner):
        return pltpu.make_async_remote_copy(
            src_ref=term_send.at[c, pl.ds((y * 2 + owner) * per + h * piece, piece)],
            dst_ref=pair_recv.at[c, y, h],
            send_sem=p_send.at[c, y, h],
            recv_sem=p_recv.at[c, y, h],
            device_id={"fac": partner},
            device_id_type=MESH,
        )

    def fac_copy(c, y, h, src):
        src_fac, src_part = split_position(src, F)
        return pltpu.make_async_remote_copy(
            src_ref=term_send.at[c, pl.ds((y * 2 + core) * per + h * piece, piece)],
            dst_ref=out.at[src_fac // 2, src_part, pl.ds(h * piece, piece), pl.ds(c * T, T)],
            send_sem=f_send.at[c, y, h],
            recv_sem=f_recv.at[c, src // 2, h],
            device_id={"fac": y * 2 + core},
            device_id_type=MESH,
        )

    def own_copy(c):
        return pltpu.make_async_copy(
            term_send.at[c, pl.ds(pos * per, per)],
            out.at[fac // 2, part, :, pl.ds(c * T, T)],
            f_send.at[c, chip, 0],
        )

    for c in range(C):

        def arrive(t, _):
            src = (me + 1 + t) % S
            str_copy(c, src, src).wait_recv()
            return 0

        lax.fori_loop(0, S - 1, arrive, 0)

        def alpha(i):
            rhs = jnp.concatenate([recv[c][aidx[s, fac, i]] for s in range(K)], axis=0)
            return jnp.dot(wa[...], rhs, preferred_element_type=jnp.float32)

        def store(i, value):
            term_send[c, pl.ds(pl.multiple_of(i * T, T), T), :] = value.astype(jnp.bfloat16)

        def for_partner(g):
            y, h = place(g)

            def block(b, _):
                i = (y * 2 + 1 - core) * (per // T) + h * (piece // T) + b
                store(i, alpha(i))
                return 0

            lax.fori_loop(0, piece // T, block, 0)
            pair_copy(c, y, h, 1 - core).start()

        def for_self(g):
            y, h = place(g)
            pair_copy(c, y, h, core).wait_recv()

            def block(b, _):
                i = (y * 2 + core) * (per // T) + h * (piece // T) + b
                other = pair_recv[c, y, h, pl.ds(pl.multiple_of(b * T, T), T), :]
                store(i, alpha(i) + other.astype(jnp.float32))
                return 0

            lax.fori_loop(0, piece // T, block, 0)

        def away(g, _):
            for_partner(g + 1)
            for_self(g)
            y, h = place(g)
            fac_copy(c, y, h, pos).start()
            return 0

        def home(g, _):
            for_partner(g + 1)
            for_self(g)
            return 0

        for_partner(0)
        lax.fori_loop(0, groups - H, away, 0)
        lax.fori_loop(groups - H, groups - 1, home, 0)
        for_self(groups - 1)
        own_copy(c).start()

    for c in range(C):

        def finish_str(t, _):
            str_copy(c, (me + 1 + t) % S, me).wait_send()
            return 0

        lax.fori_loop(0, S - 1, finish_str, 0)

        def finish_pair(g, _):
            y, h = place(g)
            pair_copy(c, y, h, 1 - core).wait_send()
            return 0

        lax.fori_loop(0, groups, finish_pair, 0)

        def finish_fac(g, _):
            y, h = place(g)
            fac_copy(c, y, h, pos).wait_send()
            fac_copy(c, y, h, y * 2 + core).wait_recv()
            return 0

        lax.fori_loop(0, groups - H, finish_fac, 0)
        own_copy(c).wait()


def local(S, F, amplitudes, beta_index, beta_tile, beta_flip, alpha_index, alpha_tile, alpha_flip, beta_tiles, alpha_tiles):
    NF, NB, K = beta_index.shape
    NT, T, _ = beta_tiles.shape
    parts, height, width = amplitudes.shape
    total = height * S
    A = height // T
    C = width // S // T
    assert F == 2 * NF and parts == 2 and NF % 2 == 0 and height % 128 == 0
    per = total // F
    H = math.gcd(per // T, 4)
    ids = (beta_index.transpose(2, 0, 1), alpha_index.transpose(2, 0, 1), beta_tile, alpha_tile)
    hbm = pl.BlockSpec(memory_space=pltpu.HBM)
    bf16 = jnp.bfloat16
    dma = pltpu.SemaphoreType.DMA
    terms = pl.pallas_call(
        functools.partial(kernel, (S, F, C, A, T, K, NB, H)),
        out_shape=jax.ShapeDtypeStruct((NF // 2, parts, per, width // S), bf16),
        in_specs=[hbm] * 9,
        out_specs=pl.BlockSpec(memory_space=pl.ANY),
        scratch_shapes=[
            pltpu.VMEM((NB, height, T), bf16),
            pltpu.VMEM((C, S, A, T, T), bf16),
            pltpu.VMEM((C, total, T), bf16),
            pltpu.VMEM((C, F // 2, H, per // H, T), bf16),
            pltpu.VMEM((K * T, T), bf16),
            pltpu.VMEM((T, K * T), bf16),
            pltpu.VMEM((NF, width), jnp.int32),
            pltpu.VMEM((NF, total), jnp.int32),
            pltpu.VMEM((NT, T, T), bf16),
            pltpu.VMEM((NT, T, T), bf16),
            pltpu.VMEM((height, T), bf16),
            pltpu.SMEM((K, NF, NB), jnp.int32),
            pltpu.SMEM((K, NF, NB), jnp.int32),
            pltpu.SMEM((NF, K), jnp.int32),
            pltpu.SMEM((NF, K), jnp.int32),
            pltpu.VMEM((height, width), bf16),
        ]
        + [pltpu.VMEM((NB, T, T), bf16) for _ in range(C)]
        + [dma((8,)), dma((8,)), dma((C, S)), dma((C, S))]
        + [dma((C, F // 2, H)) for _ in range(4)],
        compiler_params=pltpu.CompilerParams(collective_id=0, has_side_effects=True, vmem_limit_bytes=67043328),
        name="sigma",
    )(amplitudes, beta_flip, alpha_flip, beta_tiles, alpha_tiles, *ids)
    return jnp.sum(terms.astype(jnp.float32), axis=0)


def halves_kernel(dims, amp_hbm, bflip_hbm, aflip_hbm, btab_hbm, atab_hbm, bidx_hbm, aidx_hbm, btile_hbm, atile_hbm, out, far_out, *scratch):
    S, F, C, A, T, K, NB, H = dims
    amp, half_send, term_send, pair_recv, wb, wa, bflip, aflip, btab, atab, sign_a, sign_b, bidx, aidx, btile, atile, raw = scratch[:17]
    recv = scratch[17 : 16 + C]
    part_recv = scratch[16 + C : 18 + C]
    a_sem, t_sem, s_send, s_recv, p_send, p_recv, f_sem, x_sem = scratch[18 + C :]
    me = lax.axis_index("str")
    pos = lax.axis_index("fac")
    fac, part = split_position(pos, F)
    chips = F // 2
    chip = pos // 2
    core = pos % 2
    partner = chip * 2 + 1 - core
    per = term_send.shape[1] // F
    mid = S // 2
    side = me // mid
    first = side * mid
    mirror = (1 - side) * mid + me % mid
    last = C - 1

    def far(t):
        return (1 - side) * mid + (me + t) % mid

    def near(t):
        return first + (me + 1 + t) % mid

    barrier = pltpu.get_barrier_semaphore()

    def greet_str(t, _):
        pl.semaphore_signal(barrier, inc=1, device_id={"str": (me + 1 + t) % S}, device_id_type=MESH)
        return 0

    def greet_fac(t, _):
        peer = ((chip + 1 + t) % chips) * 2 + core
        pl.semaphore_signal(barrier, inc=1, device_id={"fac": peer}, device_id_type=MESH)
        pl.semaphore_signal(barrier, inc=1, device_id={"str": mirror, "fac": peer}, device_id_type=MESH)
        return 0

    lax.fori_loop(0, S - 1, greet_str, 0)
    lax.fori_loop(0, chips - 1, greet_fac, 0)
    pl.semaphore_signal(barrier, inc=1, device_id={"fac": partner}, device_id_type=MESH)

    tables = [
        pltpu.make_async_copy(src, dst, t_sem.at[n])
        for n, (src, dst) in enumerate(
            [
                (bflip_hbm, bflip),
                (aflip_hbm, aflip),
                (btile_hbm, btile),
                (bidx_hbm, bidx),
                (btab_hbm, btab),
                (atab_hbm, atab),
                (aidx_hbm, aidx),
                (atile_hbm, atile),
            ]
        )
    ]

    def load(a):
        return pltpu.make_async_copy(amp_hbm.at[part, pl.ds(a * T, T)], raw.at[pl.ds(a * T, T)], a_sem.at[a])

    for copy in tables[:5]:
        copy.start()
    for a in range(A):
        load(a).start()
    for copy in tables[5:]:
        copy.start()

    def signs(flips, start, size):
        value = flips[:, pl.ds(start, size)]
        mine = lax.broadcasted_iota(jnp.int32, value.shape, 0) == fac
        return 1 - 2 * jnp.sum(jnp.where(mine, value.astype(jnp.float32), 0.0), axis=0, keepdims=True)

    tables[0].wait()
    sign_b[...] = jnp.broadcast_to(signs(bflip, 0, NB * T), sign_b.shape).astype(jnp.bfloat16)
    tables[1].wait()
    for a in range(A):
        row = signs(aflip, pl.multiple_of((me * A + a) * T, T), T)
        sign_a[pl.ds(a * T, T), :] = jnp.broadcast_to(row, (T, T)).T.astype(jnp.bfloat16)
    tables[2].wait()
    tables[3].wait()
    tables[4].wait()
    for s in range(K):
        wb[pl.ds(s * T, T), :] = btab[btile[fac, s]].T
    for m in range(2):
        part_recv[m][mid * A] = jnp.zeros((T, T), jnp.bfloat16)

    def slot(c, q):
        return c * (S - 1) + (q - me - 1 + S) % S

    def wait_bytes(ref, sem):
        pltpu.make_async_copy(ref, ref, sem).wait()

    def str_copy(c, q):
        return pltpu.make_async_remote_copy(
            src_ref=half_send.at[slot(c, q)],
            dst_ref=recv[c].at[pl.ds(me * A, A)],
            send_sem=s_send,
            recv_sem=s_recv.at[c],
            device_id={"str": q},
            device_id_type=MESH,
        )

    def strip_copy(q, a):
        return pltpu.make_async_remote_copy(
            src_ref=half_send.at[slot(0, q), a],
            dst_ref=recv[0].at[me * A + a],
            send_sem=s_send,
            recv_sem=s_recv.at[0],
            device_id={"str": q},
            device_id_type=MESH,
        )

    def owner(m, r):
        return r if m == 0 else (1 - side) * mid + r % mid

    def part_copy(m, t):
        return pltpu.make_async_remote_copy(
            src_ref=half_send.at[last * (S - 1) + m * (mid - 1) + t],
            dst_ref=part_recv[m].at[pl.ds(me % mid * A, A)],
            send_sem=s_send,
            recv_sem=s_recv.at[last + m],
            device_id={"str": near(t)},
            device_id_type=MESH,
        )

    def sign(a):
        load(a).wait()
        rows = pl.ds(pl.multiple_of(a * T, T), T)
        row_sign = sign_a[rows, :]
        for k in range(NB):
            column = jnp.broadcast_to(sign_b[:, k * T : (k + 1) * T].reshape(1, 16, T), (T // 16, 16, T)).reshape(T, T)
            amp[k, rows, :] = raw[rows, k * T : (k + 1) * T] * column * row_sign

    def strip(a):
        rows = pl.ds(pl.multiple_of(a * T, T), T)
        blocks = [jnp.concatenate([amp[bidx[s, fac, far(t) * C], rows, :] for s in range(K)], axis=1) for t in range(mid)]
        res = jnp.dot(jnp.concatenate(blocks, axis=0), wb[...], preferred_element_type=jnp.float32).astype(jnp.bfloat16)
        for t in range(mid):
            half_send[slot(0, far(t)), a] = res[t * T : (t + 1) * T]

    def send_strip(a):
        for t in range(mid):
            strip_copy(far(t), a).start()

    sign(0)
    strip(0)
    pl.semaphore_wait(barrier, S - 1 + 2 * chips - 1)
    send_strip(0)

    def each_strip(a, _):
        sign(a)
        strip(a)
        send_strip(a)
        return 0

    lax.fori_loop(1, A, each_strip, 0)

    def beta(j):
        lhs = jnp.concatenate([amp[bidx[s, fac, j]] for s in range(K)], axis=1)
        res = jnp.dot(lhs, wb[...], preferred_element_type=jnp.float32)
        return res.astype(jnp.bfloat16).reshape(A, T, T)

    for m in (1, 0):

        def near_part(t, _):
            half_send[last * (S - 1) + m * (mid - 1) + t] = beta(owner(m, near(t)) * C + last)
            part_copy(m, t).start()
            return 0

        lax.fori_loop(0, mid - 1, near_part, 0)
        part_recv[m][pl.ds(me % mid * A, A)] = beta(owner(m, me) * C + last)

    for c in range(last):

        def to_far(t, _):
            q = far(t)
            half_send[slot(c, q)] = beta(q * C + c)
            str_copy(c, q).start()
            return 0

        def to_near(t, _):
            q = near(t)
            half_send[slot(c, q)] = beta(q * C + c)
            str_copy(c, q).start()
            return 0

        if c > 0:
            lax.fori_loop(0, mid, to_far, 0)
        lax.fori_loop(0, mid - 1, to_near, 0)
        recv[c][pl.ds(me * A, A)] = beta(me * C + c)

    for copy in tables[5:]:
        copy.wait()
    for s in range(K):
        wa[:, pl.ds(s * T, T)] = atab[atile[fac, s]]

    piece = per // H
    groups = chips * H

    def place(g):
        return (chip + 1 + g // H) % chips, g % H

    def turn(u):
        return {C: 0, last: 1}.get(u, u + 2)

    def pair_copy(u, y, h, owner_core):
        return pltpu.make_async_remote_copy(
            src_ref=term_send.at[u, pl.ds((y * 2 + owner_core) * per + h * piece, piece)],
            dst_ref=pair_recv.at[u, y, h],
            send_sem=p_send,
            recv_sem=p_recv.at[turn(u) % 2, y, h],
            device_id={"fac": partner},
            device_id_type=MESH,
        )

    def fac_copy(c, y, h):
        return pltpu.make_async_remote_copy(
            src_ref=term_send.at[c, pl.ds((y * 2 + core) * per + h * piece, piece)],
            dst_ref=out.at[fac // 2, part, pl.ds(h * piece, piece), pl.ds(c * T, T)],
            send_sem=f_sem.at[0],
            recv_sem=f_sem.at[1],
            device_id={"fac": y * 2 + core},
            device_id_type=MESH,
        )

    def far_copy(y, h):
        return pltpu.make_async_remote_copy(
            src_ref=term_send.at[C, pl.ds((y * 2 + core) * per + h * piece, piece)],
            dst_ref=far_out.at[fac // 2, part, pl.ds(h * piece, piece)],
            send_sem=x_sem.at[0],
            recv_sem=x_sem.at[1],
            device_id={"str": mirror, "fac": y * 2 + core},
            device_id_type=MESH,
        )

    def stage(u, gather, send, sent):
        def alpha(i):
            return jnp.dot(wa[...], gather(i), preferred_element_type=jnp.float32)

        def store(i, value):
            term_send[u, pl.ds(pl.multiple_of(i * T, T), T), :] = value.astype(jnp.bfloat16)

        def for_partner(g):
            y, h = place(g)

            def block(b, _):
                i = (y * 2 + 1 - core) * (per // T) + h * (piece // T) + b
                store(i, alpha(i))
                return 0

            lax.fori_loop(0, piece // T, block, 0)
            pair_copy(u, y, h, 1 - core).start()

        def for_self(g, home):
            y, h = place(g)
            pair_copy(u, y, h, core).wait_recv()

            def block(b, _):
                i = (y * 2 + core) * (per // T) + h * (piece // T) + b
                other = pair_recv[u, y, h, pl.ds(pl.multiple_of(b * T, T), T), :]
                value = alpha(i) + other.astype(jnp.float32)
                if home:
                    rows = pl.ds(pl.multiple_of(h * piece + b * T, T), T)
                    out[fac // 2, part, rows, u * T : (u + 1) * T] = value.astype(jnp.bfloat16)
                else:
                    store(i, value)
                return 0

            lax.fori_loop(0, piece // T, block, 0)

        def away(g, _):
            for_partner(g + 1)
            for_self(g, False)
            y, h = place(g)
            send(y, h).start()
            return 0

        def home(g, _):
            for_partner(g + 1)
            for_self(g, True)
            return 0

        for_partner(0)
        lax.fori_loop(0, min(sent, groups - 1), away, 0)
        if sent < groups:
            lax.fori_loop(sent, groups - 1, home, 0)
            for_self(groups - 1, True)
        else:
            for_self(groups - 1, False)
            y, h = place(groups - 1)
            send(y, h).start()

    def gather_part(m):
        def gather(i):
            blocks = []
            for s in range(K):
                k = aidx[s, fac, i] - first * A
                blocks.append(part_recv[m][jnp.where((k >= 0) & (k < mid * A), k, mid * A)])
            return jnp.concatenate(blocks, axis=0)

        return gather

    def gather_full(c):
        return lambda i: jnp.concatenate([recv[c][aidx[s, fac, i]] for s in range(K)], axis=0)

    for m in (1, 0):
        wait_bytes(part_recv[m].at[pl.ds(0, (mid - 1) * A)], s_recv.at[last + m])
        if m == 1:
            stage(C, gather_part(1), far_copy, groups)
        else:
            stage(last, gather_part(0), lambda y, h: fac_copy(last, y, h), groups - H)

    for c in range(last):
        wait_bytes(recv[c].at[pl.ds(0, (S - 1) * A)], s_recv.at[c])
        stage(c, gather_full(c), lambda y, h: fac_copy(c, y, h), groups - H)

    wait_bytes(half_send, s_send)
    wait_bytes(pair_recv, p_send)
    for n in range(2):
        wait_bytes(pair_recv.at[pl.ds(0, C), pl.ds(0, chips - 1)], f_sem.at[n])
        wait_bytes(pair_recv.at[0], x_sem.at[n])


def finish_kernel(T, rows, terms, far, out, wide, sem):
    slots, parts, per, width = terms.shape
    count = per // rows

    def copy(p, r):
        block = pl.ds(pl.multiple_of(r * rows, rows), rows)
        return pltpu.make_async_copy(wide.at[p, block], out.at[p, block], sem.at[p, r])

    for p in range(parts):

        def convert(r, _):
            block = pl.ds(pl.multiple_of(r * rows, rows), rows)
            value = sum(terms[n, p, block, :].astype(jnp.float32) for n in range(slots))
            tail = sum(far[n, p, block, :].astype(jnp.float32) for n in range(slots))
            wide[p, block, : width - T] = value[:, : width - T]
            wide[p, block, width - T :] = value[:, width - T :] + tail
            copy(p, r).start()
            return 0

        lax.fori_loop(0, count, convert, 0)

    for p in range(parts):

        def wait(r, _):
            copy(p, r).wait()
            return 0

        lax.fori_loop(0, count, wait, 0)


def halves(S, F, amplitudes, beta_index, beta_tile, beta_flip, alpha_index, alpha_tile, alpha_flip, beta_tiles, alpha_tiles):
    NF, NB, K = beta_index.shape
    NT, T, _ = beta_tiles.shape
    parts, height, width = amplitudes.shape
    total = height * S
    A = height // T
    C = width // S // T
    mid = S // 2
    assert F == 2 * NF and parts == 2 and NF % 2 == 0 and height % T == 0 and S % 2 == 0
    per = total // F
    H = math.gcd(per // T, 4)
    ids = (beta_index.transpose(2, 0, 1), alpha_index.transpose(2, 0, 1), beta_tile, alpha_tile)
    hbm = pl.BlockSpec(memory_space=pltpu.HBM)
    vmem = pl.BlockSpec(memory_space=pltpu.VMEM)
    bf16 = jnp.bfloat16
    dma = pltpu.SemaphoreType.DMA
    terms, far = pl.pallas_call(
        functools.partial(halves_kernel, (S, F, C, A, T, K, NB, H)),
        out_shape=(
            pltpu.VMEM((NF // 2, parts, per, width // S), bf16),
            pltpu.VMEM((NF // 2, parts, per, T), bf16),
        ),
        in_specs=[hbm] * 9,
        out_specs=(vmem, vmem),
        scratch_shapes=[
            pltpu.VMEM((NB, height, T), bf16),
            pltpu.VMEM(((C - 1) * (S - 1) + 2 * (mid - 1), A, T, T), bf16),
            pltpu.VMEM((C + 1, total, T), bf16),
            pltpu.VMEM((C + 1, F // 2, H, per // H, T), bf16),
            pltpu.VMEM((K * T, T), bf16),
            pltpu.VMEM((T, K * T), bf16),
            pltpu.VMEM((NF, width), jnp.int32),
            pltpu.VMEM((NF, total), jnp.int32),
            pltpu.VMEM((NT, T, T), bf16),
            pltpu.VMEM((NT, T, T), bf16),
            pltpu.VMEM((height, T), bf16),
            pltpu.VMEM((16, width), bf16),
            pltpu.SMEM((K, NF, NB), jnp.int32),
            pltpu.SMEM((K, NF, NB), jnp.int32),
            pltpu.SMEM((NF, K), jnp.int32),
            pltpu.SMEM((NF, K), jnp.int32),
            pltpu.VMEM((height, width), bf16),
        ]
        + [pltpu.VMEM((NB, T, T), bf16) for _ in range(C - 1)]
        + [pltpu.VMEM((mid * A + 1, T, T), bf16) for _ in range(2)]
        + [dma((A,)), dma((8,)), dma, dma((C + 1,)), dma, dma((2, F // 2, H)), dma((2,)), dma((2,))],
        compiler_params=pltpu.CompilerParams(collective_id=0, has_side_effects=True, vmem_limit_bytes=48 << 20),
        name="sigma",
    )(*[pltpu.with_memory_space_constraint(x, pltpu.HBM) for x in (amplitudes, beta_flip, alpha_flip, beta_tiles, alpha_tiles, *ids)])
    rows = math.gcd(per, 128)
    return pl.pallas_call(
        functools.partial(finish_kernel, T, rows),
        out_shape=jax.ShapeDtypeStruct((parts, per, width // S), jnp.float32),
        in_specs=[vmem, vmem],
        out_specs=pl.BlockSpec(memory_space=pltpu.HBM),
        scratch_shapes=[pltpu.VMEM((parts, per, width // S), jnp.float32), dma((parts, per // rows))],
        compiler_params=pltpu.CompilerParams(vmem_limit_bytes=16 << 20),
        name="finish",
    )(terms, far)


def either(S, F, *args):
    height, width, T = args[0].shape[1], args[0].shape[2], args[7].shape[1]
    form = halves if width // S >= 2 * T and height % T == 0 and S % 2 == 0 else local
    return form(S, F, *args)


def solution(mesh):
    return jax.shard_map(
        functools.partial(either, mesh.shape["str"], mesh.shape["fac"]),
        mesh=mesh,
        in_specs=(P(None, "str", None), P(), P(), P(), P(), P(), P(), P(), P()),
        out_specs=P(None, "fac", "str"),
        check_vma=False,
    )
```

```python
import functools
import math

import jax
import jax.numpy as jnp
from jax import lax
from jax.experimental import pallas as pl
from jax.experimental.pallas import tpu as pltpu
from jax.sharding import PartitionSpec as P

MESH = pl.DeviceIdType.MESH


def split_position(pos, F):
    factors = F // 2
    return pos % factors, pos // factors


def kernel(dims, amp_hbm, bflip_hbm, aflip_hbm, btab_hbm, atab_hbm, bidx_hbm, aidx_hbm, btile_hbm, atile_hbm, out, *scratch):
    S, F, C, A, T, K, NB, H = dims
    amp, half_send, term_send, pair_recv, wb, wa, bflip, aflip, btab, atab, sign_a, bidx, aidx, btile, atile, raw = scratch[:16]
    recv = scratch[16 : 16 + C]
    a_sem, t_sem, s_send, s_recv, p_send, p_recv, f_send, f_recv = scratch[16 + C :]
    me = lax.axis_index("str")
    pos = lax.axis_index("fac")
    fac, part = split_position(pos, F)
    chips = F // 2
    chip = pos // 2
    core = pos % 2
    per = term_send.shape[1] // F

    barrier = pltpu.get_barrier_semaphore()

    def greet_str(t, _):
        pl.semaphore_signal(barrier, inc=1, device_id={"str": (me + 1 + t) % S}, device_id_type=MESH)
        return 0

    def greet_fac(t, _):
        peer = ((chip + 1 + t) % chips) * 2 + core
        pl.semaphore_signal(barrier, inc=1, device_id={"fac": peer}, device_id_type=MESH)
        return 0

    partner = chip * 2 + 1 - core
    lax.fori_loop(0, S - 1, greet_str, 0)
    lax.fori_loop(0, chips - 1, greet_fac, 0)
    pl.semaphore_signal(barrier, inc=1, device_id={"fac": partner}, device_id_type=MESH)

    tables = [
        pltpu.make_async_copy(src, dst, t_sem.at[n])
        for n, (src, dst) in enumerate(
            [
                (bflip_hbm, bflip),
                (aflip_hbm, aflip),
                (btab_hbm, btab),
                (bidx_hbm, bidx),
                (btile_hbm, btile),
                (atab_hbm, atab),
                (aidx_hbm, aidx),
                (atile_hbm, atile),
            ]
        )
    ]

    strip = A * T // 8

    def load(k):
        return pltpu.make_async_copy(amp_hbm.at[part, pl.ds(k * strip, strip)], raw.at[pl.ds(k * strip, strip)], a_sem.at[k])

    def start_load(k, _):
        load(k).start()
        return 0

    for copy in tables[:5]:
        copy.start()
    lax.fori_loop(0, 8, start_load, 0)
    for copy in tables[5:]:
        copy.start()

    def signs(flips, block):
        value = flips[:, pl.ds(block * T if isinstance(block, int) else pl.multiple_of(block * T, T), T)].astype(jnp.float32)
        mine = lax.broadcasted_iota(jnp.int32, value.shape, 0) == fac
        return 1 - 2 * jnp.sum(jnp.where(mine, value, 0.0), axis=0, keepdims=True)

    tables[1].wait()
    for r in range(A):
        row = signs(aflip, me * A + r)
        sign_a[pl.ds(r * T, T), :] = jnp.broadcast_to(row, (T, T)).T.astype(jnp.bfloat16)
    tables[4].wait()
    tables[2].wait()
    for s in range(K):
        wb[pl.ds(s * T, T), :] = btab[btile[fac, s]].T
    tables[0].wait()
    tables[3].wait()

    def sign(r, _):
        load(r).wait()
        rows = pl.ds(pl.multiple_of(r * strip, strip), strip)
        row_sign = sign_a[rows, :]
        for k in range(NB):
            amp[k, rows, :] = raw[rows, pl.ds(k * T, T)] * signs(bflip, k).astype(jnp.bfloat16) * row_sign
        return 0

    lax.fori_loop(0, 8, sign, 0)
    pl.semaphore_wait(barrier, S - 1 + chips)

    mid = S // 2

    def dest(t):
        side = (me // mid + 1 + t // mid) % 2
        return side * mid + (me + 1 + t) % mid

    def beta(q, c):
        j = q * C + c
        lhs = jnp.concatenate([amp[bidx[s, fac, j]] for s in range(K)], axis=1)
        res = jnp.dot(lhs, wb[...], preferred_element_type=jnp.float32)
        return res.astype(jnp.bfloat16).reshape(A, T, T)

    def str_copy(c, q, src):
        return pltpu.make_async_remote_copy(
            src_ref=half_send.at[c, q],
            dst_ref=recv[c].at[pl.ds(src * A, A)],
            send_sem=s_send.at[c, q],
            recv_sem=s_recv.at[c, src],
            device_id={"str": q},
            device_id_type=MESH,
        )

    for c in range(C):

        def step(t, _):
            q = dest(t)
            half_send[c, q] = beta(q, c)
            str_copy(c, q, me).start()
            return 0

        lax.fori_loop(0, S - 1, step, 0)
        recv[c][pl.ds(me * A, A)] = beta(me, c)

    for copy in tables[5:]:
        copy.wait()
    for s in range(K):
        wa[:, pl.ds(s * T, T)] = atab[atile[fac, s]]

    piece = per // H
    groups = chips * H

    def place(g):
        return (chip + 1 + g // H) % chips, g % H

    def pair_copy(c, y, h, owner):
        return pltpu.make_async_remote_copy(
            src_ref=term_send.at[c, pl.ds((y * 2 + owner) * per + h * piece, piece)],
            dst_ref=pair_recv.at[c, y, h],
            send_sem=p_send.at[c, y, h],
            recv_sem=p_recv.at[c, y, h],
            device_id={"fac": partner},
            device_id_type=MESH,
        )

    def fac_copy(c, y, h, src):
        src_fac, src_part = split_position(src, F)
        return pltpu.make_async_remote_copy(
            src_ref=term_send.at[c, pl.ds((y * 2 + core) * per + h * piece, piece)],
            dst_ref=out.at[src_fac // 2, src_part, pl.ds(h * piece, piece), pl.ds(c * T, T)],
            send_sem=f_send.at[c, y, h],
            recv_sem=f_recv.at[c, src // 2, h],
            device_id={"fac": y * 2 + core},
            device_id_type=MESH,
        )

    def own_copy(c):
        return pltpu.make_async_copy(
            term_send.at[c, pl.ds(pos * per, per)],
            out.at[fac // 2, part, :, pl.ds(c * T, T)],
            f_send.at[c, chip, 0],
        )

    for c in range(C):

        def arrive(t, _):
            src = (me + 1 + t) % S
            str_copy(c, src, src).wait_recv()
            return 0

        lax.fori_loop(0, S - 1, arrive, 0)

        def alpha(i):
            rhs = jnp.concatenate([recv[c][aidx[s, fac, i]] for s in range(K)], axis=0)
            return jnp.dot(wa[...], rhs, preferred_element_type=jnp.float32)

        def store(i, value):
            term_send[c, pl.ds(pl.multiple_of(i * T, T), T), :] = value.astype(jnp.bfloat16)

        def for_partner(g):
            y, h = place(g)

            def block(b, _):
                i = (y * 2 + 1 - core) * (per // T) + h * (piece // T) + b
                store(i, alpha(i))
                return 0

            lax.fori_loop(0, piece // T, block, 0)
            pair_copy(c, y, h, 1 - core).start()

        def for_self(g):
            y, h = place(g)
            pair_copy(c, y, h, core).wait_recv()

            def block(b, _):
                i = (y * 2 + core) * (per // T) + h * (piece // T) + b
                other = pair_recv[c, y, h, pl.ds(pl.multiple_of(b * T, T), T), :]
                store(i, alpha(i) + other.astype(jnp.float32))
                return 0

            lax.fori_loop(0, piece // T, block, 0)

        def away(g, _):
            for_partner(g + 1)
            for_self(g)
            y, h = place(g)
            fac_copy(c, y, h, pos).start()
            return 0

        def home(g, _):
            for_partner(g + 1)
            for_self(g)
            return 0

        for_partner(0)
        lax.fori_loop(0, groups - H, away, 0)
        lax.fori_loop(groups - H, groups - 1, home, 0)
        for_self(groups - 1)
        own_copy(c).start()

    for c in range(C):

        def finish_str(t, _):
            str_copy(c, (me + 1 + t) % S, me).wait_send()
            return 0

        lax.fori_loop(0, S - 1, finish_str, 0)

        def finish_pair(g, _):
            y, h = place(g)
            pair_copy(c, y, h, 1 - core).wait_send()
            return 0

        lax.fori_loop(0, groups, finish_pair, 0)

        def finish_fac(g, _):
            y, h = place(g)
            fac_copy(c, y, h, pos).wait_send()
            fac_copy(c, y, h, y * 2 + core).wait_recv()
            return 0

        lax.fori_loop(0, groups - H, finish_fac, 0)
        own_copy(c).wait()


def local(S, F, amplitudes, beta_index, beta_tile, beta_flip, alpha_index, alpha_tile, alpha_flip, beta_tiles, alpha_tiles):
    NF, NB, K = beta_index.shape
    NT, T, _ = beta_tiles.shape
    parts, height, width = amplitudes.shape
    total = height * S
    A = height // T
    C = width // S // T
    assert F == 2 * NF and parts == 2 and NF % 2 == 0 and height % 128 == 0
    per = total // F
    H = math.gcd(per // T, 4)
    ids = (beta_index.transpose(2, 0, 1), alpha_index.transpose(2, 0, 1), beta_tile, alpha_tile)
    hbm = pl.BlockSpec(memory_space=pltpu.HBM)
    bf16 = jnp.bfloat16
    dma = pltpu.SemaphoreType.DMA
    terms = pl.pallas_call(
        functools.partial(kernel, (S, F, C, A, T, K, NB, H)),
        out_shape=jax.ShapeDtypeStruct((NF // 2, parts, per, width // S), bf16),
        in_specs=[hbm] * 9,
        out_specs=pl.BlockSpec(memory_space=pl.ANY),
        scratch_shapes=[
            pltpu.VMEM((NB, height, T), bf16),
            pltpu.VMEM((C, S, A, T, T), bf16),
            pltpu.VMEM((C, total, T), bf16),
            pltpu.VMEM((C, F // 2, H, per // H, T), bf16),
            pltpu.VMEM((K * T, T), bf16),
            pltpu.VMEM((T, K * T), bf16),
            pltpu.VMEM((NF, width), jnp.int32),
            pltpu.VMEM((NF, total), jnp.int32),
            pltpu.VMEM((NT, T, T), bf16),
            pltpu.VMEM((NT, T, T), bf16),
            pltpu.VMEM((height, T), bf16),
            pltpu.SMEM((K, NF, NB), jnp.int32),
            pltpu.SMEM((K, NF, NB), jnp.int32),
            pltpu.SMEM((NF, K), jnp.int32),
            pltpu.SMEM((NF, K), jnp.int32),
            pltpu.VMEM((height, width), bf16),
        ]
        + [pltpu.VMEM((NB, T, T), bf16) for _ in range(C)]
        + [dma((8,)), dma((8,)), dma((C, S)), dma((C, S))]
        + [dma((C, F // 2, H)) for _ in range(4)],
        compiler_params=pltpu.CompilerParams(collective_id=0, has_side_effects=True, vmem_limit_bytes=67043328),
        name="sigma",
    )(amplitudes, beta_flip, alpha_flip, beta_tiles, alpha_tiles, *ids)
    return jnp.sum(terms.astype(jnp.float32), axis=0)


def halves_kernel(dims, amp_hbm, bflip_hbm, aflip_hbm, btab_hbm, atab_hbm, bidx_hbm, aidx_hbm, btile_hbm, atile_hbm, out, far_out, *scratch):
    S, F, C, A, T, K, NB, H = dims
    amp, half_send, term_send, pair_recv, wb, wa, bflip, aflip, btab, atab, sign_a, sign_b, bidx, aidx, btile, atile, raw = scratch[:17]
    D = C // 2
    recv = scratch[17 : 17 + D]
    part_recv = (scratch[17 + D : 17 + 2 * D], scratch[17 + 2 * D : 17 + 3 * D])
    a_sem, t_sem, s_send, s_recv, p_send, p_recv, f_sem, x_sem = scratch[17 + 3 * D :]
    me = lax.axis_index("str")
    pos = lax.axis_index("fac")
    fac, part = split_position(pos, F)
    chips = F // 2
    chip = pos // 2
    core = pos % 2
    partner = chip * 2 + 1 - core
    per = term_send.shape[1] // F
    mid = S // 2
    side = me // mid
    first = side * mid
    def swap(r, t, flip):
        place = (r + mid // 2 * (1 - t % 2)) % mid
        return place + flip * (mid - 1 - 2 * place)

    def opposite(r):
        return (1 - side) * mid + (r + mid // 2) % mid

    late = (me < mid // 2) | (me >= S - mid // 2)


    def far(t):
        at = swap(me, t, t // 2) if mid == 4 else (me + t) % mid
        return (1 - side) * mid + at

    def near(t):
        at = swap(me, t, (t + 1) // 2) if mid == 4 else (me + 1 + t) % mid
        return first + at

    barrier = pltpu.get_barrier_semaphore()

    def greet_str(t, _):
        pl.semaphore_signal(barrier, inc=1, device_id={"str": (me + 1 + t) % S}, device_id_type=MESH)
        return 0

    def greet_fac(t, _):
        peer = ((chip + 1 + t) % chips) * 2 + core
        pl.semaphore_signal(barrier, inc=1, device_id={"fac": peer}, device_id_type=MESH)
        pl.semaphore_signal(barrier, inc=1, device_id={"str": opposite(me), "fac": peer}, device_id_type=MESH)
        return 0

    lax.fori_loop(0, S - 1, greet_str, 0)
    lax.fori_loop(0, chips - 1, greet_fac, 0)
    pl.semaphore_signal(barrier, inc=1, device_id={"fac": partner}, device_id_type=MESH)

    tables = [
        pltpu.make_async_copy(src, dst, t_sem.at[n])
        for n, (src, dst) in enumerate(
            [
                (bflip_hbm, bflip),
                (aflip_hbm, aflip),
                (btile_hbm, btile),
                (bidx_hbm, bidx),
                (btab_hbm, btab),
                (atab_hbm, atab),
                (aidx_hbm, aidx),
                (atile_hbm, atile),
            ]
        )
    ]

    def load(a):
        return pltpu.make_async_copy(amp_hbm.at[part, pl.ds(a * T, T)], raw.at[pl.ds(a * T, T)], a_sem.at[a])

    for copy in tables[:5]:
        copy.start()
    for a in range(A):
        load(a).start()
    for copy in tables[5:]:
        copy.start()

    def signs(flips, start, size):
        value = flips[:, pl.ds(start, size)]
        mine = lax.broadcasted_iota(jnp.int32, value.shape, 0) == fac
        return 1 - 2 * jnp.sum(jnp.where(mine, value.astype(jnp.float32), 0.0), axis=0, keepdims=True)

    tables[0].wait()
    sign_b[...] = jnp.broadcast_to(signs(bflip, 0, NB * T), sign_b.shape).astype(jnp.bfloat16)
    tables[1].wait()
    for a in range(A):
        row = signs(aflip, pl.multiple_of((me * A + a) * T, T), T)
        sign_a[pl.ds(a * T, T), :] = jnp.broadcast_to(row, (T, T)).T.astype(jnp.bfloat16)
    tables[2].wait()
    tables[3].wait()
    tables[4].wait()
    for s in range(K):
        wb[pl.ds(s * T, T), :] = btab[btile[fac, s]].T
    for m in range(2):
        for d in range(D):
            part_recv[m][d][mid * A] = jnp.zeros((T, T), jnp.bfloat16)

    def slot(c, q):
        return c * (S - 1) + (q - me - 1 + S) % S

    def wait_bytes(ref, sem):
        pltpu.make_async_copy(ref, ref, sem).wait()

    def str_copy(c, q):
        return pltpu.make_async_remote_copy(
            src_ref=half_send.at[slot(c, q)],
            dst_ref=recv[c].at[pl.ds(me * A, A)],
            send_sem=s_send,
            recv_sem=s_recv.at[c],
            device_id={"str": q},
            device_id_type=MESH,
        )

    def strip_copy(q, a):
        return pltpu.make_async_remote_copy(
            src_ref=half_send.at[slot(0, q), a],
            dst_ref=recv[0].at[me * A + a],
            send_sem=s_send,
            recv_sem=s_recv.at[0],
            device_id={"str": q},
            device_id_type=MESH,
        )

    def owner(m, r):
        return r if m == 0 else opposite(r)

    def part_slot(m, d, t):
        return D * (S - 1) + (m * D + d) * (mid - 1) + t

    def part_copy(m, d, t):
        return pltpu.make_async_remote_copy(
            src_ref=half_send.at[part_slot(m, d, t)],
            dst_ref=part_recv[m][d].at[pl.ds(me % mid * A, A)],
            send_sem=s_send,
            recv_sem=s_recv.at[D + m * D + d],
            device_id={"str": near(t)},
            device_id_type=MESH,
        )

    def sign(a):
        load(a).wait()
        rows = pl.ds(pl.multiple_of(a * T, T), T)
        row_sign = sign_a[rows, :]
        for k in range(NB):
            column = jnp.broadcast_to(sign_b[:, k * T : (k + 1) * T].reshape(1, 16, T), (T // 16, 16, T)).reshape(T, T)
            amp[k, rows, :] = raw[rows, k * T : (k + 1) * T] * column * row_sign

    def strip(a):
        rows = pl.ds(pl.multiple_of(a * T, T), T)
        blocks = [jnp.concatenate([amp[bidx[s, fac, far(t) * C], rows, :] for s in range(K)], axis=1) for t in range(mid)]
        res = jnp.dot(jnp.concatenate(blocks, axis=0), wb[...], preferred_element_type=jnp.float32).astype(jnp.bfloat16)
        for t in range(mid):
            half_send[slot(0, far(t)), a] = res[t * T : (t + 1) * T]

    def send_strip(a):
        for t in range(mid):
            strip_copy(far(t), a).start()

    sign(0)
    strip(0)
    pl.semaphore_wait(barrier, S - 1 + 2 * chips - 1)
    send_strip(0)

    def each_strip(a, _):
        sign(a)
        strip(a)
        send_strip(a)
        return 0

    lax.fori_loop(1, A, each_strip, 0)

    def beta(j):
        lhs = jnp.concatenate([amp[bidx[s, fac, j]] for s in range(K)], axis=1)
        res = jnp.dot(lhs, wb[...], preferred_element_type=jnp.float32)
        return res.astype(jnp.bfloat16).reshape(A, T, T)

    def spread_part(m, d):
        def near_part(t, _):
            half_send[part_slot(m, d, t)] = beta(owner(m, near(t)) * C + D + d)
            part_copy(m, d, t).start()
            return 0

        lax.fori_loop(0, mid - 1, near_part, 0)
        part_recv[m][d][pl.ds(me % mid * A, A)] = beta(owner(m, me) * C + D + d)

    def spread(c, dest, count):
        def one(t, _):
            q = dest(t)
            half_send[slot(c, q)] = beta(q * C + c)
            str_copy(c, q).start()
            return 0

        lax.fori_loop(0, count, one, 0)

    for d in range(D):
        spread_part(1, d)
    for c in range(D):
        if c > 0:
            spread(c, far, mid)
        spread(c, near, mid - 1)
        recv[c][pl.ds(me * A, A)] = beta(me * C + c)
    for d in range(D):
        spread_part(0, d)

    for copy in tables[5:]:
        copy.wait()
    for s in range(K):
        wa[:, pl.ds(s * T, T)] = atab[atile[fac, s]]

    piece = per // H
    groups = chips * H

    def pair_copy(u, y, h, owner_core):
        return pltpu.make_async_remote_copy(
            src_ref=term_send.at[u, pl.ds((y * 2 + owner_core) * per + h * piece, piece)],
            dst_ref=pair_recv.at[u, y, h],
            send_sem=p_send,
            recv_sem=p_recv.at[u % 2, y, h],
            device_id={"fac": partner},
            device_id_type=MESH,
        )

    def far_copy(y, h):
        return pltpu.make_async_remote_copy(
            src_ref=term_send.at[0, pl.ds((y * 2 + core) * per + h * piece, piece)],
            dst_ref=far_out.at[fac // 2, part, pl.ds(h * piece, piece)],
            send_sem=x_sem.at[0],
            recv_sem=x_sem.at[1],
            device_id={"str": opposite(me), "fac": y * 2 + core},
            device_id_type=MESH,
        )

    def columns(u):
        return slice(D * T, C * T) if u == 2 else slice(0, D * T)

    def fac_copy(u, y, h):
        return pltpu.make_async_remote_copy(
            src_ref=term_send.at[u, pl.ds((y * 2 + core) * per + h * piece, piece)],
            dst_ref=out.at[fac // 2, part, pl.ds(h * piece, piece), columns(u)],
            send_sem=f_sem.at[0],
            recv_sem=f_sem.at[1],
            device_id={"fac": y * 2 + core},
            device_id_type=MESH,
        )

    def stage(u, gather, send, sent):
        def place(g):
            return (g // H if u == 0 else (chip + 1 + g // H) % chips), g % H

        def alpha(i):
            return jnp.dot(wa[...], gather(i), preferred_element_type=jnp.float32)

        def store(i, value):
            term_send[u, pl.ds(pl.multiple_of(i * T, T), T), :] = value.astype(jnp.bfloat16)

        def for_partner(g):
            y, h = place(g)

            def block(b, _):
                i = (y * 2 + 1 - core) * (per // T) + h * (piece // T) + b
                store(i, alpha(i))
                return 0

            lax.fori_loop(0, piece // T, block, 0)
            pair_copy(u, y, h, 1 - core).start()

        def for_self(g, home):
            y, h = place(g)
            pair_copy(u, y, h, core).wait_recv()

            def block(b, _):
                i = (y * 2 + core) * (per // T) + h * (piece // T) + b
                other = pair_recv[u, y, h, pl.ds(pl.multiple_of(b * T, T), T), :]
                value = alpha(i) + other.astype(jnp.float32)
                if home:
                    rows = pl.ds(pl.multiple_of(h * piece + b * T, T), T)
                    out[fac // 2, part, rows, columns(u)] = value.astype(jnp.bfloat16)
                else:
                    store(i, value)
                return 0

            lax.fori_loop(0, piece // T, block, 0)

        def away(g, _):
            for_partner(g + 1)
            for_self(g, False)
            y, h = place(g)
            send(y, h)
            return 0

        def home(g, _):
            for_partner(g + 1)
            for_self(g, True)
            return 0

        for_partner(0)
        lax.fori_loop(0, min(sent, groups - 1), away, 0)
        if sent < groups:
            lax.fori_loop(sent, groups - 1, home, 0)
            for_self(groups - 1, True)
        else:
            for_self(groups - 1, False)
            y, h = place(groups - 1)
            send(y, h)

    def gather(buffers, index):
        columns = [jnp.concatenate([buffer[index(s)] for s in range(K)], axis=0) for buffer in buffers]
        return jnp.concatenate(columns, axis=1)

    def gather_part(m):
        def index(s, i):
            k = aidx[s, fac, i] - first * A
            return jnp.where((k >= 0) & (k < mid * A), k, mid * A)

        return lambda i: gather(part_recv[m], lambda s: index(s, i))

    for d in range(D):
        wait_bytes(part_recv[1][d].at[pl.ds(0, (mid - 1) * A)], s_recv.at[2 * D + d])


    def send_far(y, h):
        @pl.when(jnp.logical_not(late))
        def _():
            far_copy(y, h).start()

    stage(0, gather_part(1), send_far, groups)
    for c in range(D):
        wait_bytes(recv[c].at[pl.ds(0, (S - 1) * A)], s_recv.at[c])
    stage(1, lambda i: gather(recv, lambda s: aidx[s, fac, i]), lambda y, h: fac_copy(1, y, h).start(), groups - H)

    @pl.when(late)
    def _():
        def one(g, _):
            far_copy(g // H, g % H).start()
            return 0

        lax.fori_loop(0, groups, one, 0)

    for d in range(D):
        wait_bytes(part_recv[0][d].at[pl.ds(0, (mid - 1) * A)], s_recv.at[D + d])
    stage(2, gather_part(0), lambda y, h: fac_copy(2, y, h).start(), groups - H)

    wait_bytes(half_send, s_send)
    wait_bytes(pair_recv, p_send)
    for n in range(2):
        wait_bytes(pair_recv.at[pl.ds(0, 2), pl.ds(0, chips - 1)], f_sem.at[n])
        wait_bytes(pair_recv.at[0], x_sem.at[n])


def finish_kernel(rows, terms, far, out, wide, sem):
    slots, parts, per, width = terms.shape
    count = per // rows
    kept = width - far.shape[3]

    def copy(p, r):
        block = pl.ds(pl.multiple_of(r * rows, rows), rows)
        return pltpu.make_async_copy(wide.at[p, block], out.at[p, block], sem.at[p, r])

    for p in range(parts):

        def convert(r, _):
            block = pl.ds(pl.multiple_of(r * rows, rows), rows)
            value = sum(terms[n, p, block, :].astype(jnp.float32) for n in range(slots))
            tail = sum(far[n, p, block, :].astype(jnp.float32) for n in range(slots))
            wide[p, block, : kept] = value[:, : kept]
            wide[p, block, kept :] = value[:, kept :] + tail
            copy(p, r).start()
            return 0

        lax.fori_loop(0, count, convert, 0)

    for p in range(parts):

        def wait(r, _):
            copy(p, r).wait()
            return 0

        lax.fori_loop(0, count, wait, 0)


def halves(S, F, amplitudes, beta_index, beta_tile, beta_flip, alpha_index, alpha_tile, alpha_flip, beta_tiles, alpha_tiles):
    NF, NB, K = beta_index.shape
    NT, T, _ = beta_tiles.shape
    parts, height, width = amplitudes.shape
    total = height * S
    A = height // T
    C = width // S // T
    mid = S // 2
    D = C // 2
    assert C % 2 == 0
    assert F == 2 * NF and parts == 2 and NF % 2 == 0 and height % T == 0 and S % 4 == 0
    per = total // F
    H = math.gcd(per // T, 4)
    ids = (beta_index.transpose(2, 0, 1), alpha_index.transpose(2, 0, 1), beta_tile, alpha_tile)
    hbm = pl.BlockSpec(memory_space=pltpu.HBM)
    vmem = pl.BlockSpec(memory_space=pltpu.VMEM)
    bf16 = jnp.bfloat16
    dma = pltpu.SemaphoreType.DMA
    terms, far = pl.pallas_call(
        functools.partial(halves_kernel, (S, F, C, A, T, K, NB, H)),
        out_shape=(
            pltpu.VMEM((NF // 2, parts, per, width // S), bf16),
            pltpu.VMEM((NF // 2, parts, per, D * T), bf16),
        ),
        in_specs=[hbm] * 9,
        out_specs=(vmem, vmem),
        scratch_shapes=[
            pltpu.VMEM((NB, height, T), bf16),
            pltpu.VMEM((D * (S - 1) + 2 * D * (mid - 1), A, T, T), bf16),
            pltpu.VMEM((3, total, D * T), bf16),
            pltpu.VMEM((3, F // 2, H, per // H, D * T), bf16),
            pltpu.VMEM((K * T, T), bf16),
            pltpu.VMEM((T, K * T), bf16),
            pltpu.VMEM((NF, width), jnp.int32),
            pltpu.VMEM((NF, total), jnp.int32),
            pltpu.VMEM((NT, T, T), bf16),
            pltpu.VMEM((NT, T, T), bf16),
            pltpu.VMEM((height, T), bf16),
            pltpu.VMEM((16, width), bf16),
            pltpu.SMEM((K, NF, NB), jnp.int32),
            pltpu.SMEM((K, NF, NB), jnp.int32),
            pltpu.SMEM((NF, K), jnp.int32),
            pltpu.SMEM((NF, K), jnp.int32),
            pltpu.VMEM((height, width), bf16),
        ]
        + [pltpu.VMEM((NB, T, T), bf16) for _ in range(D)]
        + [pltpu.VMEM((mid * A + 1, T, T), bf16) for _ in range(2 * D)]
        + [dma((A,)), dma((8,)), dma, dma((3 * D,)), dma, dma((2, F // 2, H)), dma((2,)), dma((2,))],
        compiler_params=pltpu.CompilerParams(collective_id=0, has_side_effects=True, vmem_limit_bytes=48 << 20),
        name="sigma",
    )(*[pltpu.with_memory_space_constraint(x, pltpu.HBM) for x in (amplitudes, beta_flip, alpha_flip, beta_tiles, alpha_tiles, *ids)])
    rows = math.gcd(per, 128)
    return pl.pallas_call(
        functools.partial(finish_kernel, rows),
        out_shape=jax.ShapeDtypeStruct((parts, per, width // S), jnp.float32),
        in_specs=[vmem, vmem],
        out_specs=pl.BlockSpec(memory_space=pltpu.HBM),
        scratch_shapes=[pltpu.VMEM((parts, per, width // S), jnp.float32), dma((parts, per // rows))],
        compiler_params=pltpu.CompilerParams(vmem_limit_bytes=16 << 20),
        name="finish",
    )(terms, far)


def either(S, F, *args):
    height, width, T = args[0].shape[1], args[0].shape[2], args[7].shape[1]
    form = halves if width // S % (2 * T) == 0 and height % T == 0 and S % 4 == 0 else local
    return form(S, F, *args)


def solution(mesh):
    return jax.shard_map(
        functools.partial(either, mesh.shape["str"], mesh.shape["fac"]),
        mesh=mesh,
        in_specs=(P(None, "str", None), P(), P(), P(), P(), P(), P(), P(), P()),
        out_specs=P(None, "fac", "str"),
        check_vma=False,
    )
```

```python
import functools
import math

import jax
import jax.numpy as jnp
from jax import lax
from jax.experimental import pallas as pl
from jax.experimental.pallas import tpu as pltpu
from jax.sharding import PartitionSpec as P

MESH = pl.DeviceIdType.MESH


def split_position(pos, F):
    factors = F // 2
    return pos % factors, pos // factors


def kernel(dims, amp_hbm, bflip_hbm, aflip_hbm, btab_hbm, atab_hbm, bidx_hbm, aidx_hbm, btile_hbm, atile_hbm, out, *scratch):
    S, F, C, A, T, K, NB, H = dims
    amp, half_send, term_send, pair_recv, wb, wa, bflip, aflip, btab, atab, sign_a, bidx, aidx, btile, atile, raw = scratch[:16]
    recv = scratch[16 : 16 + C]
    a_sem, t_sem, s_send, s_recv, p_send, p_recv, f_send, f_recv = scratch[16 + C :]
    me = lax.axis_index("str")
    pos = lax.axis_index("fac")
    fac, part = split_position(pos, F)
    chips = F // 2
    chip = pos // 2
    core = pos % 2
    per = term_send.shape[1] // F

    barrier = pltpu.get_barrier_semaphore()

    def greet_str(t, _):
        pl.semaphore_signal(barrier, inc=1, device_id={"str": (me + 1 + t) % S}, device_id_type=MESH)
        return 0

    def greet_fac(t, _):
        peer = ((chip + 1 + t) % chips) * 2 + core
        pl.semaphore_signal(barrier, inc=1, device_id={"fac": peer}, device_id_type=MESH)
        return 0

    partner = chip * 2 + 1 - core
    lax.fori_loop(0, S - 1, greet_str, 0)
    lax.fori_loop(0, chips - 1, greet_fac, 0)
    pl.semaphore_signal(barrier, inc=1, device_id={"fac": partner}, device_id_type=MESH)

    tables = [
        pltpu.make_async_copy(src, dst, t_sem.at[n])
        for n, (src, dst) in enumerate(
            [
                (bflip_hbm, bflip),
                (aflip_hbm, aflip),
                (btab_hbm, btab),
                (bidx_hbm, bidx),
                (btile_hbm, btile),
                (atab_hbm, atab),
                (aidx_hbm, aidx),
                (atile_hbm, atile),
            ]
        )
    ]

    strip = A * T // 8

    def load(k):
        return pltpu.make_async_copy(amp_hbm.at[part, pl.ds(k * strip, strip)], raw.at[pl.ds(k * strip, strip)], a_sem.at[k])

    def start_load(k, _):
        load(k).start()
        return 0

    for copy in tables[:5]:
        copy.start()
    lax.fori_loop(0, 8, start_load, 0)
    for copy in tables[5:]:
        copy.start()

    def signs(flips, block):
        value = flips[:, pl.ds(block * T if isinstance(block, int) else pl.multiple_of(block * T, T), T)].astype(jnp.float32)
        mine = lax.broadcasted_iota(jnp.int32, value.shape, 0) == fac
        return 1 - 2 * jnp.sum(jnp.where(mine, value, 0.0), axis=0, keepdims=True)

    tables[1].wait()
    for r in range(A):
        row = signs(aflip, me * A + r)
        sign_a[pl.ds(r * T, T), :] = jnp.broadcast_to(row, (T, T)).T.astype(jnp.bfloat16)
    tables[4].wait()
    tables[2].wait()
    for s in range(K):
        wb[pl.ds(s * T, T), :] = btab[btile[fac, s]].T
    tables[0].wait()
    tables[3].wait()

    def sign(r, _):
        load(r).wait()
        rows = pl.ds(pl.multiple_of(r * strip, strip), strip)
        row_sign = sign_a[rows, :]
        for k in range(NB):
            amp[k, rows, :] = raw[rows, pl.ds(k * T, T)] * signs(bflip, k).astype(jnp.bfloat16) * row_sign
        return 0

    lax.fori_loop(0, 8, sign, 0)
    pl.semaphore_wait(barrier, S - 1 + chips)

    mid = S // 2

    def dest(t):
        side = (me // mid + 1 + t // mid) % 2
        return side * mid + (me + 1 + t) % mid

    def beta(q, c):
        j = q * C + c
        lhs = jnp.concatenate([amp[bidx[s, fac, j]] for s in range(K)], axis=1)
        res = jnp.dot(lhs, wb[...], preferred_element_type=jnp.float32)
        return res.astype(jnp.bfloat16).reshape(A, T, T)

    def str_copy(c, q, src):
        return pltpu.make_async_remote_copy(
            src_ref=half_send.at[c, q],
            dst_ref=recv[c].at[pl.ds(src * A, A)],
            send_sem=s_send.at[c, q],
            recv_sem=s_recv.at[c, src],
            device_id={"str": q},
            device_id_type=MESH,
        )

    for c in range(C):

        def step(t, _):
            q = dest(t)
            half_send[c, q] = beta(q, c)
            str_copy(c, q, me).start()
            return 0

        lax.fori_loop(0, S - 1, step, 0)
        recv[c][pl.ds(me * A, A)] = beta(me, c)

    for copy in tables[5:]:
        copy.wait()
    for s in range(K):
        wa[:, pl.ds(s * T, T)] = atab[atile[fac, s]]

    piece = per // H
    groups = chips * H

    def place(g):
        return (chip + 1 + g // H) % chips, g % H

    def pair_copy(c, y, h, owner):
        return pltpu.make_async_remote_copy(
            src_ref=term_send.at[c, pl.ds((y * 2 + owner) * per + h * piece, piece)],
            dst_ref=pair_recv.at[c, y, h],
            send_sem=p_send.at[c, y, h],
            recv_sem=p_recv.at[c, y, h],
            device_id={"fac": partner},
            device_id_type=MESH,
        )

    def fac_copy(c, y, h, src):
        src_fac, src_part = split_position(src, F)
        return pltpu.make_async_remote_copy(
            src_ref=term_send.at[c, pl.ds((y * 2 + core) * per + h * piece, piece)],
            dst_ref=out.at[src_fac // 2, src_part, pl.ds(h * piece, piece), pl.ds(c * T, T)],
            send_sem=f_send.at[c, y, h],
            recv_sem=f_recv.at[c, src // 2, h],
            device_id={"fac": y * 2 + core},
            device_id_type=MESH,
        )

    def own_copy(c):
        return pltpu.make_async_copy(
            term_send.at[c, pl.ds(pos * per, per)],
            out.at[fac // 2, part, :, pl.ds(c * T, T)],
            f_send.at[c, chip, 0],
        )

    for c in range(C):

        def arrive(t, _):
            src = (me + 1 + t) % S
            str_copy(c, src, src).wait_recv()
            return 0

        lax.fori_loop(0, S - 1, arrive, 0)

        def alpha(i):
            rhs = jnp.concatenate([recv[c][aidx[s, fac, i]] for s in range(K)], axis=0)
            return jnp.dot(wa[...], rhs, preferred_element_type=jnp.float32)

        def store(i, value):
            term_send[c, pl.ds(pl.multiple_of(i * T, T), T), :] = value.astype(jnp.bfloat16)

        def for_partner(g):
            y, h = place(g)

            def block(b, _):
                i = (y * 2 + 1 - core) * (per // T) + h * (piece // T) + b
                store(i, alpha(i))
                return 0

            lax.fori_loop(0, piece // T, block, 0)
            pair_copy(c, y, h, 1 - core).start()

        def for_self(g):
            y, h = place(g)
            pair_copy(c, y, h, core).wait_recv()

            def block(b, _):
                i = (y * 2 + core) * (per // T) + h * (piece // T) + b
                other = pair_recv[c, y, h, pl.ds(pl.multiple_of(b * T, T), T), :]
                store(i, alpha(i) + other.astype(jnp.float32))
                return 0

            lax.fori_loop(0, piece // T, block, 0)

        def away(g, _):
            for_partner(g + 1)
            for_self(g)
            y, h = place(g)
            fac_copy(c, y, h, pos).start()
            return 0

        def home(g, _):
            for_partner(g + 1)
            for_self(g)
            return 0

        for_partner(0)
        lax.fori_loop(0, groups - H, away, 0)
        lax.fori_loop(groups - H, groups - 1, home, 0)
        for_self(groups - 1)
        own_copy(c).start()

    for c in range(C):

        def finish_str(t, _):
            str_copy(c, (me + 1 + t) % S, me).wait_send()
            return 0

        lax.fori_loop(0, S - 1, finish_str, 0)

        def finish_pair(g, _):
            y, h = place(g)
            pair_copy(c, y, h, 1 - core).wait_send()
            return 0

        lax.fori_loop(0, groups, finish_pair, 0)

        def finish_fac(g, _):
            y, h = place(g)
            fac_copy(c, y, h, pos).wait_send()
            fac_copy(c, y, h, y * 2 + core).wait_recv()
            return 0

        lax.fori_loop(0, groups - H, finish_fac, 0)
        own_copy(c).wait()


def local(S, F, amplitudes, beta_index, beta_tile, beta_flip, alpha_index, alpha_tile, alpha_flip, beta_tiles, alpha_tiles):
    NF, NB, K = beta_index.shape
    NT, T, _ = beta_tiles.shape
    parts, height, width = amplitudes.shape
    total = height * S
    A = height // T
    C = width // S // T
    assert F == 2 * NF and parts == 2 and NF % 2 == 0 and height % 128 == 0
    per = total // F
    H = math.gcd(per // T, 4)
    ids = (beta_index.transpose(2, 0, 1), alpha_index.transpose(2, 0, 1), beta_tile, alpha_tile)
    hbm = pl.BlockSpec(memory_space=pltpu.HBM)
    bf16 = jnp.bfloat16
    dma = pltpu.SemaphoreType.DMA
    terms = pl.pallas_call(
        functools.partial(kernel, (S, F, C, A, T, K, NB, H)),
        out_shape=jax.ShapeDtypeStruct((NF // 2, parts, per, width // S), bf16),
        in_specs=[hbm] * 9,
        out_specs=pl.BlockSpec(memory_space=pl.ANY),
        scratch_shapes=[
            pltpu.VMEM((NB, height, T), bf16),
            pltpu.VMEM((C, S, A, T, T), bf16),
            pltpu.VMEM((C, total, T), bf16),
            pltpu.VMEM((C, F // 2, H, per // H, T), bf16),
            pltpu.VMEM((K * T, T), bf16),
            pltpu.VMEM((T, K * T), bf16),
            pltpu.VMEM((NF, width), jnp.int32),
            pltpu.VMEM((NF, total), jnp.int32),
            pltpu.VMEM((NT, T, T), bf16),
            pltpu.VMEM((NT, T, T), bf16),
            pltpu.VMEM((height, T), bf16),
            pltpu.SMEM((K, NF, NB), jnp.int32),
            pltpu.SMEM((K, NF, NB), jnp.int32),
            pltpu.SMEM((NF, K), jnp.int32),
            pltpu.SMEM((NF, K), jnp.int32),
            pltpu.VMEM((height, width), bf16),
        ]
        + [pltpu.VMEM((NB, T, T), bf16) for _ in range(C)]
        + [dma((8,)), dma((8,)), dma((C, S)), dma((C, S))]
        + [dma((C, F // 2, H)) for _ in range(4)],
        compiler_params=pltpu.CompilerParams(collective_id=0, has_side_effects=True, vmem_limit_bytes=67043328),
        name="sigma",
    )(amplitudes, beta_flip, alpha_flip, beta_tiles, alpha_tiles, *ids)
    return jnp.sum(terms.astype(jnp.float32), axis=0)


def halves_kernel(dims, amp_hbm, bflip_hbm, aflip_hbm, btab_hbm, atab_hbm, bidx_hbm, aidx_hbm, btile_hbm, atile_hbm, out, far_out, *scratch):
    S, F, C, A, T, K, NB, H = dims
    amp, half_send, term_send, pair_recv, wb, wa, bflip, aflip, btab, atab, sign_a, sign_b, bidx, aidx, btile, atile, raw = scratch[:17]
    D = C // 2
    recv = scratch[17 : 17 + D]
    part_recv = (scratch[17 + D : 17 + 2 * D], scratch[17 + 2 * D : 17 + 3 * D])
    a_sem, t_sem, s_send, s_recv, p_send, p_recv, f_sem, x_sem = scratch[17 + 3 * D :]
    me = lax.axis_index("str")
    pos = lax.axis_index("fac")
    fac, part = split_position(pos, F)
    chips = F // 2
    chip = pos // 2
    core = pos % 2
    partner = chip * 2 + 1 - core
    per = term_send.shape[1] // F
    mid = S // 2
    side = me // mid
    first = side * mid
    def swap(r, t, flip):
        place = (r + mid // 2 * (1 - t % 2)) % mid
        return place + flip * (mid - 1 - 2 * place)

    def opposite(r):
        return (1 - side) * mid + (r + mid // 2) % mid

    late = (me < mid // 2) | (me >= S - mid // 2)


    def far(t):
        at = swap(me, t + 1, t // 2) if mid == 4 else (me + t) % mid
        return (1 - side) * mid + at

    def near(t):
        at = swap(me, t, (t + 1) // 2) if mid == 4 else (me + 1 + t) % mid
        return first + at

    barrier = pltpu.get_barrier_semaphore()

    def greet_str(t, _):
        pl.semaphore_signal(barrier, inc=1, device_id={"str": (me + 1 + t) % S}, device_id_type=MESH)
        return 0

    def greet_fac(t, _):
        peer = ((chip + 1 + t) % chips) * 2 + core
        pl.semaphore_signal(barrier, inc=1, device_id={"fac": peer}, device_id_type=MESH)
        pl.semaphore_signal(barrier, inc=1, device_id={"str": opposite(me), "fac": peer}, device_id_type=MESH)
        return 0

    lax.fori_loop(0, S - 1, greet_str, 0)
    lax.fori_loop(0, chips - 1, greet_fac, 0)
    pl.semaphore_signal(barrier, inc=1, device_id={"fac": partner}, device_id_type=MESH)

    tables = [
        pltpu.make_async_copy(src, dst, t_sem.at[n])
        for n, (src, dst) in enumerate(
            [
                (bflip_hbm, bflip),
                (aflip_hbm, aflip),
                (btile_hbm, btile),
                (bidx_hbm, bidx),
                (btab_hbm, btab),
                (atab_hbm, atab),
                (aidx_hbm, aidx),
                (atile_hbm, atile),
            ]
        )
    ]

    def load(a):
        return pltpu.make_async_copy(amp_hbm.at[part, pl.ds(a * T, T)], raw.at[pl.ds(a * T, T)], a_sem.at[a])

    for copy in tables[:5]:
        copy.start()
    load(0).start()

    def signs(flips, start, size):
        value = flips[:, pl.ds(start, size)]
        mine = lax.broadcasted_iota(jnp.int32, value.shape, 0) == fac
        return 1 - 2 * jnp.sum(jnp.where(mine, value.astype(jnp.float32), 0.0), axis=0, keepdims=True)

    tables[0].wait()
    sign_b[...] = jnp.broadcast_to(signs(bflip, 0, NB * T), sign_b.shape).astype(jnp.bfloat16)
    tables[1].wait()
    for a in range(A):
        row = signs(aflip, pl.multiple_of((me * A + a) * T, T), T)
        sign_a[pl.ds(a * T, T), :] = jnp.broadcast_to(row, (T, T)).T.astype(jnp.bfloat16)
    tables[2].wait()
    tables[3].wait()
    tables[4].wait()
    for s in range(K):
        wb[pl.ds(s * T, T), :] = btab[btile[fac, s]].T
    for m in range(2):
        for d in range(D):
            part_recv[m][d][mid * A] = jnp.zeros((T, T), jnp.bfloat16)

    def slot(c, q):
        return c * (S - 1) + (q - me - 1 + S) % S

    def wait_bytes(ref, sem):
        pltpu.make_async_copy(ref, ref, sem).wait()

    def str_copy(c, q):
        return pltpu.make_async_remote_copy(
            src_ref=half_send.at[slot(c, q)],
            dst_ref=recv[c].at[pl.ds(me * A, A)],
            send_sem=s_send,
            recv_sem=s_recv.at[c],
            device_id={"str": q},
            device_id_type=MESH,
        )

    def strip_copy(q, a):
        return pltpu.make_async_remote_copy(
            src_ref=half_send.at[slot(0, q), a],
            dst_ref=recv[0].at[me * A + a],
            send_sem=s_send,
            recv_sem=s_recv.at[0],
            device_id={"str": q},
            device_id_type=MESH,
        )

    def owner(m, r):
        return r if m == 0 else opposite(r)

    def part_slot(m, d, t):
        return D * (S - 1) + (m * D + d) * (mid - 1) + t

    def part_copy(m, d, t):
        return pltpu.make_async_remote_copy(
            src_ref=half_send.at[part_slot(m, d, t)],
            dst_ref=part_recv[m][d].at[pl.ds(me % mid * A, A)],
            send_sem=s_send,
            recv_sem=s_recv.at[D + m * D + d],
            device_id={"str": near(t)},
            device_id_type=MESH,
        )

    def sign(a):
        rows = pl.ds(pl.multiple_of(a * T, T), T)
        row_sign = sign_a[rows, :]
        for k in range(NB):
            column = jnp.broadcast_to(sign_b[:, k * T : (k + 1) * T].reshape(1, 16, T), (T // 16, 16, T)).reshape(T, T)
            amp[k, rows, :] = raw[rows, k * T : (k + 1) * T] * column * row_sign

    def strip(a):
        rows = pl.ds(pl.multiple_of(a * T, T), T)
        blocks = [jnp.concatenate([amp[bidx[s, fac, far(t) * C], rows, :] for s in range(K)], axis=1) for t in range(mid)]
        res = jnp.dot(jnp.concatenate(blocks, axis=0), wb[...], preferred_element_type=jnp.float32).astype(jnp.bfloat16)
        for t in range(mid):
            half_send[slot(0, far(t)), a] = res[t * T : (t + 1) * T]

    def send_strip(a):
        for t in range(mid):
            strip_copy(far(t), a).start()

    load(0).wait()
    for a in range(1, A):
        load(a).start()
    for copy in tables[5:]:
        copy.start()
    sign(0)
    strip(0)
    pl.semaphore_wait(barrier, S - 1 + 2 * chips - 1)
    send_strip(0)

    def each_strip(a, _):
        load(a).wait()
        sign(a)
        strip(a)
        send_strip(a)
        return 0

    lax.fori_loop(1, A, each_strip, 0)

    def beta(j):
        lhs = jnp.concatenate([amp[bidx[s, fac, j]] for s in range(K)], axis=1)
        res = jnp.dot(lhs, wb[...], preferred_element_type=jnp.float32)
        return res.astype(jnp.bfloat16).reshape(A, T, T)

    def spread_part(m, d):
        def near_part(t, _):
            half_send[part_slot(m, d, t)] = beta(owner(m, near(t)) * C + D + d)
            part_copy(m, d, t).start()
            return 0

        lax.fori_loop(0, mid - 1, near_part, 0)
        part_recv[m][d][pl.ds(me % mid * A, A)] = beta(owner(m, me) * C + D + d)

    def spread(c, dest, count):
        def one(t, _):
            q = dest(t)
            half_send[slot(c, q)] = beta(q * C + c)
            str_copy(c, q).start()
            return 0

        lax.fori_loop(0, count, one, 0)

    for d in range(D):
        spread_part(1, d)
    for c in range(D):
        if c > 0:
            spread(c, far, mid)
        spread(c, near, mid - 1)
        recv[c][pl.ds(me * A, A)] = beta(me * C + c)
    for d in range(D):
        spread_part(0, d)

    for copy in tables[5:]:
        copy.wait()
    for s in range(K):
        wa[:, pl.ds(s * T, T)] = atab[atile[fac, s]]

    piece = per // H
    groups = chips * H

    def pair_copy(u, y, h, owner_core):
        return pltpu.make_async_remote_copy(
            src_ref=term_send.at[u, pl.ds((y * 2 + owner_core) * per + h * piece, piece)],
            dst_ref=pair_recv.at[u, y, h],
            send_sem=p_send,
            recv_sem=p_recv.at[u % 2, y, h],
            device_id={"fac": partner},
            device_id_type=MESH,
        )

    def far_copy(y, h):
        return pltpu.make_async_remote_copy(
            src_ref=term_send.at[0, pl.ds((y * 2 + core) * per + h * piece, piece)],
            dst_ref=far_out.at[fac // 2, part, pl.ds(h * piece, piece)],
            send_sem=x_sem.at[0],
            recv_sem=x_sem.at[1],
            device_id={"str": opposite(me), "fac": y * 2 + core},
            device_id_type=MESH,
        )

    def columns(u):
        return slice(D * T, C * T) if u == 2 else slice(0, D * T)

    def fac_copy(u, y, h):
        return pltpu.make_async_remote_copy(
            src_ref=term_send.at[u, pl.ds((y * 2 + core) * per + h * piece, piece)],
            dst_ref=out.at[fac // 2, part, pl.ds(h * piece, piece), columns(u)],
            send_sem=f_sem.at[0],
            recv_sem=f_sem.at[1],
            device_id={"fac": y * 2 + core},
            device_id_type=MESH,
        )

    def stage(u, gather, send, sent):
        def place(g):
            return (g // H if u == 0 else (chip + 1 + g // H) % chips), g % H

        def alpha(i):
            return jnp.dot(wa[...], gather(i), preferred_element_type=jnp.float32)

        def store(i, value):
            term_send[u, pl.ds(pl.multiple_of(i * T, T), T), :] = value.astype(jnp.bfloat16)

        def for_partner(g):
            y, h = place(g)

            def block(b, _):
                i = (y * 2 + 1 - core) * (per // T) + h * (piece // T) + b
                store(i, alpha(i))
                return 0

            lax.fori_loop(0, piece // T, block, 0)
            pair_copy(u, y, h, 1 - core).start()

        def for_self(g, home):
            y, h = place(g)
            pair_copy(u, y, h, core).wait_recv()

            def block(b, _):
                i = (y * 2 + core) * (per // T) + h * (piece // T) + b
                other = pair_recv[u, y, h, pl.ds(pl.multiple_of(b * T, T), T), :]
                value = alpha(i) + other.astype(jnp.float32)
                if home:
                    rows = pl.ds(pl.multiple_of(h * piece + b * T, T), T)
                    out[fac // 2, part, rows, columns(u)] = value.astype(jnp.bfloat16)
                else:
                    store(i, value)
                return 0

            lax.fori_loop(0, piece // T, block, 0)

        def away(g, _):
            for_partner(g + 1)
            for_self(g, False)
            y, h = place(g)
            send(y, h)
            return 0

        def home(g, _):
            for_partner(g + 1)
            for_self(g, True)
            return 0

        for_partner(0)
        lax.fori_loop(0, min(sent, groups - 1), away, 0)
        if sent < groups:
            lax.fori_loop(sent, groups - 1, home, 0)
            for_self(groups - 1, True)
        else:
            for_self(groups - 1, False)
            y, h = place(groups - 1)
            send(y, h)

    def gather(buffers, index):
        columns = [jnp.concatenate([buffer[index(s)] for s in range(K)], axis=0) for buffer in buffers]
        return jnp.concatenate(columns, axis=1)

    def gather_part(m):
        def index(s, i):
            k = aidx[s, fac, i] - first * A
            return jnp.where((k >= 0) & (k < mid * A), k, mid * A)

        return lambda i: gather(part_recv[m], lambda s: index(s, i))

    for d in range(D):
        wait_bytes(part_recv[1][d].at[pl.ds(0, (mid - 1) * A)], s_recv.at[2 * D + d])


    def send_far(y, h):
        @pl.when(jnp.logical_not(late))
        def _():
            far_copy(y, h).start()

    stage(0, gather_part(1), send_far, groups)
    for c in range(D):
        wait_bytes(recv[c].at[pl.ds(0, (S - 1) * A)], s_recv.at[c])
    stage(1, lambda i: gather(recv, lambda s: aidx[s, fac, i]), lambda y, h: fac_copy(1, y, h).start(), groups - H)

    @pl.when(late)
    def _():
        def one(g, _):
            far_copy(g // H, g % H).start()
            return 0

        lax.fori_loop(0, groups, one, 0)

    for d in range(D):
        wait_bytes(part_recv[0][d].at[pl.ds(0, (mid - 1) * A)], s_recv.at[D + d])
    stage(2, gather_part(0), lambda y, h: fac_copy(2, y, h).start(), groups - H)

    wait_bytes(half_send, s_send)
    wait_bytes(pair_recv, p_send)
    for n in range(2):
        wait_bytes(pair_recv.at[pl.ds(0, 2), pl.ds(0, chips - 1)], f_sem.at[n])
        wait_bytes(pair_recv.at[0], x_sem.at[n])


def finish_kernel(rows, terms, far, out, wide, sem):
    slots, parts, per, width = terms.shape
    count = per // rows
    kept = width - far.shape[3]

    def copy(p, r):
        block = pl.ds(pl.multiple_of(r * rows, rows), rows)
        return pltpu.make_async_copy(wide.at[p, block], out.at[p, block], sem)

    for p in range(parts):

        def convert(r, _):
            block = pl.ds(pl.multiple_of(r * rows, rows), rows)
            value = sum(terms[n, p, block, :].astype(jnp.float32) for n in range(slots))
            tail = sum(far[n, p, block, :].astype(jnp.float32) for n in range(slots))
            wide[p, block, : kept] = value[:, : kept]
            wide[p, block, kept :] = value[:, kept :] + tail
            copy(p, r).start()
            return 0

        lax.fori_loop(0, count, convert, 0)

    pltpu.make_async_copy(wide, out, sem).wait()


def halves(S, F, amplitudes, beta_index, beta_tile, beta_flip, alpha_index, alpha_tile, alpha_flip, beta_tiles, alpha_tiles):
    NF, NB, K = beta_index.shape
    NT, T, _ = beta_tiles.shape
    parts, height, width = amplitudes.shape
    total = height * S
    A = height // T
    C = width // S // T
    mid = S // 2
    D = C // 2
    assert C % 2 == 0
    assert F == 2 * NF and parts == 2 and NF % 2 == 0 and height % T == 0 and S % 4 == 0
    per = total // F
    H = math.gcd(per // T, 4)
    ids = (beta_index.transpose(2, 0, 1), alpha_index.transpose(2, 0, 1), beta_tile, alpha_tile)
    hbm = pl.BlockSpec(memory_space=pltpu.HBM)
    vmem = pl.BlockSpec(memory_space=pltpu.VMEM)
    bf16 = jnp.bfloat16
    dma = pltpu.SemaphoreType.DMA
    terms, far = pl.pallas_call(
        functools.partial(halves_kernel, (S, F, C, A, T, K, NB, H)),
        out_shape=(
            pltpu.VMEM((NF // 2, parts, per, width // S), bf16),
            pltpu.VMEM((NF // 2, parts, per, D * T), bf16),
        ),
        in_specs=[hbm] * 9,
        out_specs=(vmem, vmem),
        scratch_shapes=[
            pltpu.VMEM((NB, height, T), bf16),
            pltpu.VMEM((D * (S - 1) + 2 * D * (mid - 1), A, T, T), bf16),
            pltpu.VMEM((3, total, D * T), bf16),
            pltpu.VMEM((3, F // 2, H, per // H, D * T), bf16),
            pltpu.VMEM((K * T, T), bf16),
            pltpu.VMEM((T, K * T), bf16),
            pltpu.VMEM((NF, width), jnp.int32),
            pltpu.VMEM((NF, total), jnp.int32),
            pltpu.VMEM((NT, T, T), bf16),
            pltpu.VMEM((NT, T, T), bf16),
            pltpu.VMEM((height, T), bf16),
            pltpu.VMEM((16, width), bf16),
            pltpu.SMEM((K, NF, NB), jnp.int32),
            pltpu.SMEM((K, NF, NB), jnp.int32),
            pltpu.SMEM((NF, K), jnp.int32),
            pltpu.SMEM((NF, K), jnp.int32),
            pltpu.VMEM((height, width), bf16),
        ]
        + [pltpu.VMEM((NB, T, T), bf16) for _ in range(D)]
        + [pltpu.VMEM((mid * A + 1, T, T), bf16) for _ in range(2 * D)]
        + [dma((A,)), dma((8,)), dma, dma((3 * D,)), dma, dma((2, F // 2, H)), dma((2,)), dma((2,))],
        compiler_params=pltpu.CompilerParams(collective_id=0, has_side_effects=True, vmem_limit_bytes=48 << 20),
        name="sigma",
    )(*[pltpu.with_memory_space_constraint(x, pltpu.HBM) for x in (amplitudes, beta_flip, alpha_flip, beta_tiles, alpha_tiles, *ids)])
    rows = math.gcd(per, 128)
    return pl.pallas_call(
        functools.partial(finish_kernel, rows),
        out_shape=jax.ShapeDtypeStruct((parts, per, width // S), jnp.float32),
        in_specs=[vmem, vmem],
        out_specs=pl.BlockSpec(memory_space=pltpu.HBM),
        scratch_shapes=[pltpu.VMEM((parts, per, width // S), jnp.float32), dma],
        compiler_params=pltpu.CompilerParams(vmem_limit_bytes=16 << 20),
        name="finish",
    )(terms, far)


def either(S, F, *args):
    height, width, T = args[0].shape[1], args[0].shape[2], args[7].shape[1]
    form = halves if width // S % (2 * T) == 0 and height % T == 0 and S % 4 == 0 else local
    return form(S, F, *args)


def solution(mesh):
    return jax.shard_map(
        functools.partial(either, mesh.shape["str"], mesh.shape["fac"]),
        mesh=mesh,
        in_specs=(P(None, "str", None), P(), P(), P(), P(), P(), P(), P(), P()),
        out_specs=P(None, "fac", "str"),
        check_vma=False,
    )
```

```python
import functools
import math

import jax
import jax.numpy as jnp
from jax import lax
from jax.experimental import pallas as pl
from jax.experimental.pallas import tpu as pltpu
from jax.sharding import PartitionSpec as P

MESH = pl.DeviceIdType.MESH


def split_position(pos, F):
    factors = F // 2
    return pos % factors, pos // factors


def kernel(dims, amp_hbm, bflip_hbm, aflip_hbm, btab_hbm, atab_hbm, bidx_hbm, aidx_hbm, btile_hbm, atile_hbm, out, *scratch):
    S, F, C, A, T, K, NB, H = dims
    amp, half_send, term_send, pair_recv, wb, wa, bflip, aflip, btab, atab, sign_a, bidx, aidx, btile, atile, raw = scratch[:16]
    recv = scratch[16 : 16 + C]
    a_sem, t_sem, s_send, s_recv, p_send, p_recv, f_send, f_recv = scratch[16 + C :]
    me = lax.axis_index("str")
    pos = lax.axis_index("fac")
    fac, part = split_position(pos, F)
    chips = F // 2
    chip = pos // 2
    core = pos % 2
    per = term_send.shape[1] // F

    barrier = pltpu.get_barrier_semaphore()

    def greet_str(t, _):
        pl.semaphore_signal(barrier, inc=1, device_id={"str": (me + 1 + t) % S}, device_id_type=MESH)
        return 0

    def greet_fac(t, _):
        peer = ((chip + 1 + t) % chips) * 2 + core
        pl.semaphore_signal(barrier, inc=1, device_id={"fac": peer}, device_id_type=MESH)
        return 0

    partner = chip * 2 + 1 - core
    lax.fori_loop(0, S - 1, greet_str, 0)
    lax.fori_loop(0, chips - 1, greet_fac, 0)
    pl.semaphore_signal(barrier, inc=1, device_id={"fac": partner}, device_id_type=MESH)

    tables = [
        pltpu.make_async_copy(src, dst, t_sem.at[n])
        for n, (src, dst) in enumerate(
            [
                (bflip_hbm, bflip),
                (aflip_hbm, aflip),
                (btab_hbm, btab),
                (bidx_hbm, bidx),
                (btile_hbm, btile),
                (atab_hbm, atab),
                (aidx_hbm, aidx),
                (atile_hbm, atile),
            ]
        )
    ]

    strip = A * T // 8

    def load(k):
        return pltpu.make_async_copy(amp_hbm.at[part, pl.ds(k * strip, strip)], raw.at[pl.ds(k * strip, strip)], a_sem.at[k])

    def start_load(k, _):
        load(k).start()
        return 0

    for copy in tables[:5]:
        copy.start()
    lax.fori_loop(0, 8, start_load, 0)
    for copy in tables[5:]:
        copy.start()

    def signs(flips, block):
        value = flips[:, pl.ds(block * T if isinstance(block, int) else pl.multiple_of(block * T, T), T)].astype(jnp.float32)
        mine = lax.broadcasted_iota(jnp.int32, value.shape, 0) == fac
        return 1 - 2 * jnp.sum(jnp.where(mine, value, 0.0), axis=0, keepdims=True)

    tables[1].wait()
    for r in range(A):
        row = signs(aflip, me * A + r)
        sign_a[pl.ds(r * T, T), :] = jnp.broadcast_to(row, (T, T)).T.astype(jnp.bfloat16)
    tables[4].wait()
    tables[2].wait()
    for s in range(K):
        wb[pl.ds(s * T, T), :] = btab[btile[fac, s]].T
    tables[0].wait()
    tables[3].wait()

    def sign(r, _):
        load(r).wait()
        rows = pl.ds(pl.multiple_of(r * strip, strip), strip)
        row_sign = sign_a[rows, :]
        for k in range(NB):
            amp[k, rows, :] = raw[rows, pl.ds(k * T, T)] * signs(bflip, k).astype(jnp.bfloat16) * row_sign
        return 0

    lax.fori_loop(0, 8, sign, 0)
    pl.semaphore_wait(barrier, S - 1 + chips)

    mid = S // 2

    def dest(t):
        side = (me // mid + 1 + t // mid) % 2
        return side * mid + (me + 1 + t) % mid

    def beta(q, c):
        j = q * C + c
        lhs = jnp.concatenate([amp[bidx[s, fac, j]] for s in range(K)], axis=1)
        res = jnp.dot(lhs, wb[...], preferred_element_type=jnp.float32)
        return res.astype(jnp.bfloat16).reshape(A, T, T)

    def str_copy(c, q, src):
        return pltpu.make_async_remote_copy(
            src_ref=half_send.at[c, q],
            dst_ref=recv[c].at[pl.ds(src * A, A)],
            send_sem=s_send.at[c, q],
            recv_sem=s_recv.at[c, src],
            device_id={"str": q},
            device_id_type=MESH,
        )

    for c in range(C):

        def step(t, _):
            q = dest(t)
            half_send[c, q] = beta(q, c)
            str_copy(c, q, me).start()
            return 0

        lax.fori_loop(0, S - 1, step, 0)
        recv[c][pl.ds(me * A, A)] = beta(me, c)

    for copy in tables[5:]:
        copy.wait()
    for s in range(K):
        wa[:, pl.ds(s * T, T)] = atab[atile[fac, s]]

    piece = per // H
    groups = chips * H

    def place(g):
        return (chip + 1 + g // H) % chips, g % H

    def pair_copy(c, y, h, owner):
        return pltpu.make_async_remote_copy(
            src_ref=term_send.at[c, pl.ds((y * 2 + owner) * per + h * piece, piece)],
            dst_ref=pair_recv.at[c, y, h],
            send_sem=p_send.at[c, y, h],
            recv_sem=p_recv.at[c, y, h],
            device_id={"fac": partner},
            device_id_type=MESH,
        )

    def fac_copy(c, y, h, src):
        src_fac, src_part = split_position(src, F)
        return pltpu.make_async_remote_copy(
            src_ref=term_send.at[c, pl.ds((y * 2 + core) * per + h * piece, piece)],
            dst_ref=out.at[src_fac // 2, src_part, pl.ds(h * piece, piece), pl.ds(c * T, T)],
            send_sem=f_send.at[c, y, h],
            recv_sem=f_recv.at[c, src // 2, h],
            device_id={"fac": y * 2 + core},
            device_id_type=MESH,
        )

    def own_copy(c):
        return pltpu.make_async_copy(
            term_send.at[c, pl.ds(pos * per, per)],
            out.at[fac // 2, part, :, pl.ds(c * T, T)],
            f_send.at[c, chip, 0],
        )

    for c in range(C):

        def arrive(t, _):
            src = (me + 1 + t) % S
            str_copy(c, src, src).wait_recv()
            return 0

        lax.fori_loop(0, S - 1, arrive, 0)

        def alpha(i):
            rhs = jnp.concatenate([recv[c][aidx[s, fac, i]] for s in range(K)], axis=0)
            return jnp.dot(wa[...], rhs, preferred_element_type=jnp.float32)

        def store(i, value):
            term_send[c, pl.ds(pl.multiple_of(i * T, T), T), :] = value.astype(jnp.bfloat16)

        def for_partner(g):
            y, h = place(g)

            def block(b, _):
                i = (y * 2 + 1 - core) * (per // T) + h * (piece // T) + b
                store(i, alpha(i))
                return 0

            lax.fori_loop(0, piece // T, block, 0)
            pair_copy(c, y, h, 1 - core).start()

        def for_self(g):
            y, h = place(g)
            pair_copy(c, y, h, core).wait_recv()

            def block(b, _):
                i = (y * 2 + core) * (per // T) + h * (piece // T) + b
                other = pair_recv[c, y, h, pl.ds(pl.multiple_of(b * T, T), T), :]
                store(i, alpha(i) + other.astype(jnp.float32))
                return 0

            lax.fori_loop(0, piece // T, block, 0)

        def away(g, _):
            for_partner(g + 1)
            for_self(g)
            y, h = place(g)
            fac_copy(c, y, h, pos).start()
            return 0

        def home(g, _):
            for_partner(g + 1)
            for_self(g)
            return 0

        for_partner(0)
        lax.fori_loop(0, groups - H, away, 0)
        lax.fori_loop(groups - H, groups - 1, home, 0)
        for_self(groups - 1)
        own_copy(c).start()

    for c in range(C):

        def finish_str(t, _):
            str_copy(c, (me + 1 + t) % S, me).wait_send()
            return 0

        lax.fori_loop(0, S - 1, finish_str, 0)

        def finish_pair(g, _):
            y, h = place(g)
            pair_copy(c, y, h, 1 - core).wait_send()
            return 0

        lax.fori_loop(0, groups, finish_pair, 0)

        def finish_fac(g, _):
            y, h = place(g)
            fac_copy(c, y, h, pos).wait_send()
            fac_copy(c, y, h, y * 2 + core).wait_recv()
            return 0

        lax.fori_loop(0, groups - H, finish_fac, 0)
        own_copy(c).wait()


def local(S, F, amplitudes, beta_index, beta_tile, beta_flip, alpha_index, alpha_tile, alpha_flip, beta_tiles, alpha_tiles):
    NF, NB, K = beta_index.shape
    NT, T, _ = beta_tiles.shape
    parts, height, width = amplitudes.shape
    total = height * S
    A = height // T
    C = width // S // T
    assert F == 2 * NF and parts == 2 and NF % 2 == 0 and height % 128 == 0
    per = total // F
    H = math.gcd(per // T, 4)
    ids = (beta_index.transpose(2, 0, 1), alpha_index.transpose(2, 0, 1), beta_tile, alpha_tile)
    hbm = pl.BlockSpec(memory_space=pltpu.HBM)
    bf16 = jnp.bfloat16
    dma = pltpu.SemaphoreType.DMA
    terms = pl.pallas_call(
        functools.partial(kernel, (S, F, C, A, T, K, NB, H)),
        out_shape=jax.ShapeDtypeStruct((NF // 2, parts, per, width // S), bf16),
        in_specs=[hbm] * 9,
        out_specs=pl.BlockSpec(memory_space=pl.ANY),
        scratch_shapes=[
            pltpu.VMEM((NB, height, T), bf16),
            pltpu.VMEM((C, S, A, T, T), bf16),
            pltpu.VMEM((C, total, T), bf16),
            pltpu.VMEM((C, F // 2, H, per // H, T), bf16),
            pltpu.VMEM((K * T, T), bf16),
            pltpu.VMEM((T, K * T), bf16),
            pltpu.VMEM((NF, width), jnp.int32),
            pltpu.VMEM((NF, total), jnp.int32),
            pltpu.VMEM((NT, T, T), bf16),
            pltpu.VMEM((NT, T, T), bf16),
            pltpu.VMEM((height, T), bf16),
            pltpu.SMEM((K, NF, NB), jnp.int32),
            pltpu.SMEM((K, NF, NB), jnp.int32),
            pltpu.SMEM((NF, K), jnp.int32),
            pltpu.SMEM((NF, K), jnp.int32),
            pltpu.VMEM((height, width), bf16),
        ]
        + [pltpu.VMEM((NB, T, T), bf16) for _ in range(C)]
        + [dma((8,)), dma((8,)), dma((C, S)), dma((C, S))]
        + [dma((C, F // 2, H)) for _ in range(4)],
        compiler_params=pltpu.CompilerParams(collective_id=0, has_side_effects=True, vmem_limit_bytes=67043328),
        name="sigma",
    )(amplitudes, beta_flip, alpha_flip, beta_tiles, alpha_tiles, *ids)
    return jnp.sum(terms.astype(jnp.float32), axis=0)


def halves_kernel(dims, amp_hbm, bflip_hbm, aflip_hbm, btab_hbm, atab_hbm, bidx_hbm, aidx_hbm, btile_hbm, atile_hbm, out, far_out, *scratch):
    S, F, C, A, T, K, NB, H = dims
    amp, half_send, term_send, pair_recv, wb, wa, bflip, aflip, btab, atab, sign_a, sign_b, bidx, aidx, btile, atile, raw = scratch[:17]
    D = C // 2
    recv = scratch[17 : 17 + D]
    part_recv = (scratch[17 + D : 17 + 2 * D], scratch[17 + 2 * D : 17 + 3 * D])
    a_sem, t_sem, s_send, s_recv, p_send, p_recv, f_sem, x_sem = scratch[17 + 3 * D :]
    me = lax.axis_index("str")
    pos = lax.axis_index("fac")
    fac, part = split_position(pos, F)
    chips = F // 2
    chip = pos // 2
    core = pos % 2
    partner = chip * 2 + 1 - core
    per = term_send.shape[1] // F
    mid = S // 2
    side = me // mid
    first = side * mid
    def swap(r, t, flip):
        place = (r + mid // 2 * (1 - t % 2)) % mid
        return place + flip * (mid - 1 - 2 * place)

    def opposite(r):
        return (1 - side) * mid + (r + mid // 2) % mid

    late = (me < mid // 2) | (me >= S - mid // 2)


    def far(t):
        at = swap(me, t + 1, t // 2) if mid == 4 else (me + t) % mid
        return (1 - side) * mid + at

    def near(t):
        at = swap(me, t, (t + 1) // 2) if mid == 4 else (me + 1 + t) % mid
        return first + at

    barrier = pltpu.get_barrier_semaphore()

    def greet_str(t, _):
        pl.semaphore_signal(barrier, inc=1, device_id={"str": (me + 1 + (t + mid - 1) % (S - 1)) % S}, device_id_type=MESH)
        return 0

    def greet_fac(t, _):
        peer = ((chip + 1 + t) % chips) * 2 + core
        pl.semaphore_signal(barrier, inc=1, device_id={"fac": peer}, device_id_type=MESH)
        pl.semaphore_signal(barrier, inc=1, device_id={"str": opposite(me), "fac": peer}, device_id_type=MESH)
        return 0

    lax.fori_loop(0, S - 1, greet_str, 0)
    lax.fori_loop(0, chips - 1, greet_fac, 0)
    pl.semaphore_signal(barrier, inc=1, device_id={"fac": partner}, device_id_type=MESH)

    tables = [
        pltpu.make_async_copy(src, dst, t_sem.at[n])
        for n, (src, dst) in enumerate(
            [
                (bflip_hbm, bflip),
                (aflip_hbm, aflip),
                (btile_hbm, btile),
                (bidx_hbm, bidx),
                (btab_hbm, btab),
                (atab_hbm, atab),
                (aidx_hbm, aidx),
                (atile_hbm, atile),
            ]
        )
    ]

    def load(a, n):
        rows = pl.ds(a * T, n * T)
        return pltpu.make_async_copy(amp_hbm.at[part, rows], raw.at[rows], a_sem.at[a])

    for copy in tables[:5]:
        copy.start()
    load(0, 1).start()

    def signs(flips, start, size):
        value = flips[:, pl.ds(start, size)]
        mine = lax.broadcasted_iota(jnp.int32, value.shape, 0) == fac
        return 1 - 2 * jnp.sum(jnp.where(mine, value.astype(jnp.float32), 0.0), axis=0, keepdims=True)

    tables[0].wait()
    sign_b[...] = jnp.broadcast_to(signs(bflip, 0, NB * T), sign_b.shape).astype(jnp.bfloat16)
    tables[1].wait()
    for a in range(A):
        row = signs(aflip, pl.multiple_of((me * A + a) * T, T), T)
        sign_a[pl.ds(a * T, T), :] = jnp.broadcast_to(row, (T, T)).T.astype(jnp.bfloat16)
    tables[2].wait()
    tables[3].wait()
    tables[4].wait()
    for s in range(K):
        wb[pl.ds(s * T, T), :] = btab[btile[fac, s]].T
    for m in range(2):
        for d in range(D):
            part_recv[m][d][mid * A] = jnp.zeros((T, T), jnp.bfloat16)

    def slot(c, q):
        return c * (S - 1) + (q - me - 1 + S) % S

    def wait_bytes(ref, sem):
        pltpu.make_async_copy(ref, ref, sem).wait()

    def str_copy(c, q):
        return pltpu.make_async_remote_copy(
            src_ref=half_send.at[slot(c, q)],
            dst_ref=recv[c].at[pl.ds(me * A, A)],
            send_sem=s_send,
            recv_sem=s_recv.at[c],
            device_id={"str": q},
            device_id_type=MESH,
        )

    def strip_copy(q, a):
        return pltpu.make_async_remote_copy(
            src_ref=half_send.at[slot(0, q), a],
            dst_ref=recv[0].at[me * A + a],
            send_sem=s_send,
            recv_sem=s_recv.at[0],
            device_id={"str": q},
            device_id_type=MESH,
        )

    def owner(m, r):
        return r if m == 0 else opposite(r)

    def part_slot(m, d, t):
        return D * (S - 1) + (m * D + d) * (mid - 1) + t

    def part_copy(m, d, t):
        return pltpu.make_async_remote_copy(
            src_ref=half_send.at[part_slot(m, d, t)],
            dst_ref=part_recv[m][d].at[pl.ds(me % mid * A, A)],
            send_sem=s_send,
            recv_sem=s_recv.at[D + m * D + d],
            device_id={"str": near(t)},
            device_id_type=MESH,
        )

    def sign(a):
        rows = pl.ds(pl.multiple_of(a * T, T), T)
        row_sign = sign_a[rows, :]
        for k in range(NB):
            column = jnp.broadcast_to(sign_b[:, k * T : (k + 1) * T].reshape(1, 16, T), (T // 16, 16, T)).reshape(T, T)
            amp[k, rows, :] = raw[rows, k * T : (k + 1) * T] * column * row_sign

    def strip(a):
        rows = pl.ds(pl.multiple_of(a * T, T), T)
        blocks = [jnp.concatenate([amp[bidx[s, fac, far(t) * C], rows, :] for s in range(K)], axis=1) for t in range(mid)]
        res = jnp.dot(jnp.concatenate(blocks, axis=0), wb[...], preferred_element_type=jnp.float32).astype(jnp.bfloat16)
        for t in range(mid):
            half_send[slot(0, far(t)), a] = res[t * T : (t + 1) * T]

    def send_strip(a):
        for t in range(mid):
            strip_copy(far(t), a).start()

    load(0, 1).wait()
    load(1, A - 1).start()
    for copy in tables[5:]:
        copy.start()
    sign(0)
    strip(0)
    pl.semaphore_wait(barrier, S - 1 + 2 * chips - 1)
    send_strip(0)

    def each_strip(a, _):
        sign(a)
        strip(a)
        send_strip(a)
        return 0

    load(1, A - 1).wait()
    lax.fori_loop(1, A, each_strip, 0)

    def beta(j):
        lhs = jnp.concatenate([amp[bidx[s, fac, j]] for s in range(K)], axis=1)
        res = jnp.dot(lhs, wb[...], preferred_element_type=jnp.float32)
        return res.astype(jnp.bfloat16).reshape(A, T, T)

    def spread_part(m, d):
        def near_part(t, _):
            half_send[part_slot(m, d, t)] = beta(owner(m, near(t)) * C + D + d)
            part_copy(m, d, t).start()
            return 0

        lax.fori_loop(0, mid - 1, near_part, 0)
        part_recv[m][d][pl.ds(me % mid * A, A)] = beta(owner(m, me) * C + D + d)

    def spread(c, dest, count):
        def one(t, _):
            q = dest(t)
            half_send[slot(c, q)] = beta(q * C + c)
            str_copy(c, q).start()
            return 0

        lax.fori_loop(0, count, one, 0)

    for d in range(D):
        spread_part(1, d)
    for c in range(D):
        if c > 0:
            spread(c, far, mid)
        spread(c, near, mid - 1)
        recv[c][pl.ds(me * A, A)] = beta(me * C + c)
    for d in range(D):
        spread_part(0, d)

    for copy in tables[5:]:
        copy.wait()
    for s in range(K):
        wa[:, pl.ds(s * T, T)] = atab[atile[fac, s]]

    piece = per // H
    groups = chips * H

    def pair_copy(u, y, h, owner_core):
        return pltpu.make_async_remote_copy(
            src_ref=term_send.at[u, pl.ds((y * 2 + owner_core) * per + h * piece, piece)],
            dst_ref=pair_recv.at[u, y, h],
            send_sem=p_send,
            recv_sem=p_recv.at[u % 2, y, h],
            device_id={"fac": partner},
            device_id_type=MESH,
        )

    def far_copy(y, h):
        return pltpu.make_async_remote_copy(
            src_ref=term_send.at[0, pl.ds((y * 2 + core) * per + h * piece, piece)],
            dst_ref=far_out.at[fac // 2, part, pl.ds(h * piece, piece)],
            send_sem=x_sem.at[0],
            recv_sem=x_sem.at[1],
            device_id={"str": opposite(me), "fac": y * 2 + core},
            device_id_type=MESH,
        )

    def columns(u):
        return slice(D * T, C * T) if u == 2 else slice(0, D * T)

    def fac_copy(u, y, h):
        return pltpu.make_async_remote_copy(
            src_ref=term_send.at[u, pl.ds((y * 2 + core) * per + h * piece, piece)],
            dst_ref=out.at[fac // 2, part, pl.ds(h * piece, piece), columns(u)],
            send_sem=f_sem.at[0],
            recv_sem=f_sem.at[1],
            device_id={"fac": y * 2 + core},
            device_id_type=MESH,
        )

    def stage(u, gather, send, sent):
        def place(g):
            return (g // H if u == 0 else (chip + 1 + g // H) % chips), g % H

        def alpha(i):
            return jnp.dot(wa[...], gather(i), preferred_element_type=jnp.float32)

        def store(i, value):
            term_send[u, pl.ds(pl.multiple_of(i * T, T), T), :] = value.astype(jnp.bfloat16)

        def for_partner(g):
            y, h = place(g)

            def block(b, _):
                i = (y * 2 + 1 - core) * (per // T) + h * (piece // T) + b
                store(i, alpha(i))
                return 0

            lax.fori_loop(0, piece // T, block, 0)
            pair_copy(u, y, h, 1 - core).start()

        def for_self(g, home):
            y, h = place(g)
            pair_copy(u, y, h, core).wait_recv()

            def block(b, _):
                i = (y * 2 + core) * (per // T) + h * (piece // T) + b
                other = pair_recv[u, y, h, pl.ds(pl.multiple_of(b * T, T), T), :]
                value = alpha(i) + other.astype(jnp.float32)
                if home:
                    rows = pl.ds(pl.multiple_of(h * piece + b * T, T), T)
                    out[fac // 2, part, rows, columns(u)] = value.astype(jnp.bfloat16)
                else:
                    store(i, value)
                return 0

            lax.fori_loop(0, piece // T, block, 0)

        def away(g, _):
            for_partner(g + 1)
            for_self(g, False)
            y, h = place(g)
            send(y, h)
            return 0

        def home(g, _):
            for_partner(g + 1)
            for_self(g, True)
            return 0

        for_partner(0)
        lax.fori_loop(0, min(sent, groups - 1), away, 0)
        if sent < groups:
            lax.fori_loop(sent, groups - 1, home, 0)
            for_self(groups - 1, True)
        else:
            for_self(groups - 1, False)
            y, h = place(groups - 1)
            send(y, h)

    def gather(buffers, index):
        columns = [jnp.concatenate([buffer[index(s)] for s in range(K)], axis=0) for buffer in buffers]
        return jnp.concatenate(columns, axis=1)

    def gather_part(m):
        def index(s, i):
            k = aidx[s, fac, i] - first * A
            return jnp.where((k >= 0) & (k < mid * A), k, mid * A)

        return lambda i: gather(part_recv[m], lambda s: index(s, i))

    for d in range(D):
        wait_bytes(part_recv[1][d].at[pl.ds(0, (mid - 1) * A)], s_recv.at[2 * D + d])


    def send_far(y, h):
        @pl.when(jnp.logical_not(late))
        def _():
            far_copy(y, h).start()

    stage(0, gather_part(1), send_far, groups)
    for c in range(D):
        wait_bytes(recv[c].at[pl.ds(0, (S - 1) * A)], s_recv.at[c])
    stage(1, lambda i: gather(recv, lambda s: aidx[s, fac, i]), lambda y, h: fac_copy(1, y, h).start(), groups - H)

    @pl.when(late)
    def _():
        def one(g, _):
            far_copy(g // H, g % H).start()
            return 0

        lax.fori_loop(0, groups, one, 0)

    for d in range(D):
        wait_bytes(part_recv[0][d].at[pl.ds(0, (mid - 1) * A)], s_recv.at[D + d])
    stage(2, gather_part(0), lambda y, h: fac_copy(2, y, h).start(), groups - H)

    wait_bytes(half_send, s_send)
    wait_bytes(pair_recv, p_send)
    for n in range(2):
        wait_bytes(pair_recv.at[pl.ds(0, 2), pl.ds(0, chips - 1)], f_sem.at[n])
        wait_bytes(pair_recv.at[0], x_sem.at[n])


def finish_kernel(rows, terms, far, out, wide, sem):
    slots, parts, per, width = terms.shape
    count = per // rows
    kept = width - far.shape[3]

    def copy(p, r):
        block = pl.ds(pl.multiple_of(r * rows, rows), rows)
        return pltpu.make_async_copy(wide.at[p, block], out.at[p, block], sem)

    for p in range(parts):

        def convert(r, _):
            block = pl.ds(pl.multiple_of(r * rows, rows), rows)
            value = sum(terms[n, p, block, :].astype(jnp.float32) for n in range(slots))
            tail = sum(far[n, p, block, :].astype(jnp.float32) for n in range(slots))
            wide[p, block, : kept] = value[:, : kept]
            wide[p, block, kept :] = value[:, kept :] + tail
            copy(p, r).start()
            return 0

        lax.fori_loop(0, count, convert, 0)

    pltpu.make_async_copy(wide, out, sem).wait()


def halves(S, F, amplitudes, beta_index, beta_tile, beta_flip, alpha_index, alpha_tile, alpha_flip, beta_tiles, alpha_tiles):
    NF, NB, K = beta_index.shape
    NT, T, _ = beta_tiles.shape
    parts, height, width = amplitudes.shape
    total = height * S
    A = height // T
    C = width // S // T
    mid = S // 2
    D = C // 2
    assert C % 2 == 0
    assert F == 2 * NF and parts == 2 and NF % 2 == 0 and height % T == 0 and S % 4 == 0
    per = total // F
    H = math.gcd(per // T, 2)
    ids = (beta_index.transpose(2, 0, 1), alpha_index.transpose(2, 0, 1), beta_tile, alpha_tile)
    hbm = pl.BlockSpec(memory_space=pltpu.HBM)
    vmem = pl.BlockSpec(memory_space=pltpu.VMEM)
    bf16 = jnp.bfloat16
    dma = pltpu.SemaphoreType.DMA
    terms, far = pl.pallas_call(
        functools.partial(halves_kernel, (S, F, C, A, T, K, NB, H)),
        out_shape=(
            pltpu.VMEM((NF // 2, parts, per, width // S), bf16),
            pltpu.VMEM((NF // 2, parts, per, D * T), bf16),
        ),
        in_specs=[hbm] * 9,
        out_specs=(vmem, vmem),
        scratch_shapes=[
            pltpu.VMEM((NB, height, T), bf16),
            pltpu.VMEM((D * (S - 1) + 2 * D * (mid - 1), A, T, T), bf16),
            pltpu.VMEM((3, total, D * T), bf16),
            pltpu.VMEM((3, F // 2, H, per // H, D * T), bf16),
            pltpu.VMEM((K * T, T), bf16),
            pltpu.VMEM((T, K * T), bf16),
            pltpu.VMEM((NF, width), jnp.int32),
            pltpu.VMEM((NF, total), jnp.int32),
            pltpu.VMEM((NT, T, T), bf16),
            pltpu.VMEM((NT, T, T), bf16),
            pltpu.VMEM((height, T), bf16),
            pltpu.VMEM((16, width), bf16),
            pltpu.SMEM((K, NF, NB), jnp.int32),
            pltpu.SMEM((K, NF, NB), jnp.int32),
            pltpu.SMEM((NF, K), jnp.int32),
            pltpu.SMEM((NF, K), jnp.int32),
            pltpu.VMEM((height, width), bf16),
        ]
        + [pltpu.VMEM((NB, T, T), bf16) for _ in range(D)]
        + [pltpu.VMEM((mid * A + 1, T, T), bf16) for _ in range(2 * D)]
        + [dma((2,)), dma((8,)), dma, dma((3 * D,)), dma, dma((2, F // 2, H)), dma((2,)), dma((2,))],
        compiler_params=pltpu.CompilerParams(collective_id=0, has_side_effects=True, vmem_limit_bytes=48 << 20),
        name="sigma",
    )(*[pltpu.with_memory_space_constraint(x, pltpu.HBM) for x in (amplitudes, beta_flip, alpha_flip, beta_tiles, alpha_tiles, *ids)])
    rows = math.gcd(per, 128)
    return pl.pallas_call(
        functools.partial(finish_kernel, rows),
        out_shape=jax.ShapeDtypeStruct((parts, per, width // S), jnp.float32),
        in_specs=[vmem, vmem],
        out_specs=pl.BlockSpec(memory_space=pltpu.HBM),
        scratch_shapes=[pltpu.VMEM((parts, per, width // S), jnp.float32), dma],
        compiler_params=pltpu.CompilerParams(vmem_limit_bytes=16 << 20),
        name="finish",
    )(terms, far)


def either(S, F, *args):
    height, width, T = args[0].shape[1], args[0].shape[2], args[7].shape[1]
    form = halves if width // S % (2 * T) == 0 and height >= 2 * T and height % T == 0 and S % 4 == 0 else local
    return form(S, F, *args)


def solution(mesh):
    return jax.shard_map(
        functools.partial(either, mesh.shape["str"], mesh.shape["fac"]),
        mesh=mesh,
        in_specs=(P(None, "str", None), P(), P(), P(), P(), P(), P(), P(), P()),
        out_specs=P(None, "fac", "str"),
        check_vma=False,
    )
```
